128 devices in a mesh: heads: 8 (over z, core), keys: 16 (over x, y).
Axes of the slice: x: 4, y: 4, z: 4, core: 2. Of those that a mesh axis runs over, the one named last changes fastest.
Arguments:
- queries: bfloat16 [4096, 4096], P('keys', 'heads')
- key_states: bfloat16 [131072, 4096], P('keys', 'heads')
- value_states: bfloat16 [131072, 4096], P('keys', 'heads'), may hold values from -6 to 6
- block_ids: int32 [32, 3072], P('heads', 'keys'), may hold values from 0 to 2047, as said below
- block_counts: int32 [32, 16], P('heads', 'keys'), may hold values from 2 to 192, as said below
- out_weight: bfloat16 [4096, 4096], P('heads'), may hold values from -0.09375 to 0.09375
Outputs:
- projected: bfloat16 [4096, 4096], P('keys', 'heads')
The draws below stay inside these ranges and needn't reach their ends.
Inputs may be any that keep to these rules, and one draw needn't show every extreme that they name: `block_ids`: entry h, r * 192 + j names query block b // 64 and tile b % 64 of key range r for head h; the first block_counts[h, r] entries of a head and key range are distinct, the rest are ignored; every query block is named by a counted entry of every head. `block_counts`: some head and key range has exactly 192 counted entries.
All inputs are finite; a program needn't handle non-finite values.
Results may differ from the reference program's by a relative error of at most 0.025.
Values may be sent and summed in bfloat16 or wider, within the bound.
No kernel may reach another device: no remote copies, remote signals or barrier semaphores. Data moves between devices by JAX's collectives and lax.ppermute only.
A program may use at most 192 MiB of HBM per device.

```python
import jax
import jax.numpy as jnp
from jax import lax

HEADS = 32
HEAD_DIM = 128
D = 4096
BLOCK = 128
Q_LEN = 4096
CTX = 131072
QBLOCKS = 32
KTILES = 64
LBLK = 2048
CAP = 192
COVER = 2
N_KEYS = 16


def listed_blocks(key):
    high_count = jax.random.randint(jax.random.fold_in(key, 101), (HEADS, 1), max(COVER, CAP // 10), CAP + 1)
    low_count = jnp.maximum(COVER, high_count // 2)
    raw_draw = jax.random.randint(jax.random.fold_in(key, 102), (HEADS, N_KEYS), 0, 1 << 20)
    counts = low_count + raw_draw % (high_count - low_count + 1)
    full_head = jax.random.randint(jax.random.fold_in(key, 103), (), 0, HEADS)
    full_range = jax.random.randint(jax.random.fold_in(key, 104), (), 0, N_KEYS)
    counts = counts.at[full_head, full_range].set(CAP)
    slot_keys = jax.random.split(jax.random.fold_in(key, 105), HEADS * N_KEYS)
    ranges = jnp.tile(jnp.arange(N_KEYS, dtype=jnp.int32), HEADS)

    def one_list(slot_key, range_index):
        cover_tile = jax.random.randint(jax.random.fold_in(slot_key, 1), (COVER,), 0, KTILES)
        cover_query = (range_index + jnp.arange(COVER, dtype=jnp.int32) * N_KEYS) % QBLOCKS
        cover_ids = (cover_query * KTILES + cover_tile).astype(jnp.int32)
        shuffled = jax.random.permutation(jax.random.fold_in(slot_key, 2), LBLK).astype(jnp.int32)
        is_cover = jnp.any(shuffled[:, None] == cover_ids[None, :], axis=1).astype(jnp.int32)
        reorder = jnp.argsort(is_cover, stable=True)
        remainder = shuffled[reorder][:CAP - COVER]
        return jnp.concatenate([cover_ids, remainder])
    listed = jax.vmap(one_list)(slot_keys, ranges).reshape(HEADS, N_KEYS, CAP)
    return (listed.astype(jnp.int32), counts.astype(jnp.int32))


def draw_block_ids(key, part):
    listed, counts = listed_blocks(key)
    return listed.reshape(HEADS, N_KEYS * CAP)


def draw_block_counts(key, part):
    listed, counts = listed_blocks(key)
    return counts


def draw_queries(key, part):
    base_key = jax.random.fold_in(key, 301)
    values = jax.random.truncated_normal(base_key, -4.0, 4.0, (Q_LEN, D)) * 2.5
    return values.astype(jnp.bfloat16)


def draw_key_states(key, part):
    base_key = jax.random.fold_in(key, 311)
    values = jax.random.truncated_normal(base_key, -4.0, 4.0, (CTX, D))
    return values.astype(jnp.bfloat16)


def steps_of(own_key, extent, shards, smallest, largest):
    def one(axis_at, blocks):
        draws = jax.random.uniform(jax.random.fold_in(jax.random.fold_in(own_key, 6), axis_at), (blocks,), jnp.float32, smallest / len(shards), largest / len(shards))
        return jnp.repeat(jnp.exp(draws), extent[axis_at] // blocks).reshape((-1,) + (1,) * (len(extent) - axis_at - 1))

    loudness = one(*shards[0])
    for cut in shards[1:]:
        loudness = loudness * one(*cut)
    return loudness


def normal_values(rng, extent, width, limit, pieces=(), held_as=jnp.bfloat16):
    drawn = width * jax.random.normal(rng, extent, jnp.float32)
    if pieces:
        drawn = drawn * steps_of(rng, extent, pieces, -0.22, 0.18)
    return jnp.clip(drawn, -limit, limit).astype(held_as)


def setup_inputs(seed: int = 0) -> dict:
    key_of = jax.random.split(jax.random.key(seed), 7)
    queries = draw_queries(jax.random.fold_in(key_of[6], 71), 0)
    key_states = draw_key_states(jax.random.fold_in(key_of[6], 71), 0)
    value_states = normal_values(key_of[2], (CTX, D), 1.0, 6.0, ((0, 16), (1, 8)))
    block_ids = draw_block_ids(jax.random.fold_in(key_of[6], 71), 0)
    block_counts = draw_block_counts(jax.random.fold_in(key_of[6], 71), 0)
    out_weight = normal_values(key_of[5], (D, D), D ** -0.5, 0.09375, ((0, 8),))
    return dict(queries=queries, key_states=key_states, value_states=value_states, block_ids=block_ids, block_counts=block_counts, out_weight=out_weight)


def head_attention(packed):
    query_h, key_h, value_h, ids_h, count_h = packed
    query_tile = ids_h // KTILES
    key_tile = ids_h % KTILES + (jnp.arange(N_KEYS, dtype=jnp.int32) * KTILES)[:, None]
    live_slot = jnp.arange(CAP, dtype=jnp.int32)[None, :] < count_h[:, None]
    query_blocks = query_h.astype(jnp.float32).reshape(QBLOCKS, BLOCK, HEAD_DIM)[query_tile]
    key_blocks = key_h.astype(jnp.float32).reshape(N_KEYS * KTILES, BLOCK, HEAD_DIM)[key_tile]
    value_blocks = value_h.astype(jnp.float32).reshape(N_KEYS * KTILES, BLOCK, HEAD_DIM)[key_tile]
    scores = jnp.einsum("rcid,rcjd->rcij", query_blocks, key_blocks) * (HEAD_DIM ** -0.5)
    block_best = jnp.where(live_slot[:, :, None], scores.max(-1), -jnp.inf)
    one_hot = query_tile[:, :, None] == jnp.arange(QBLOCKS, dtype=jnp.int32)[None, None, :]
    row_max = jnp.where(one_hot[..., None], block_best[:, :, None, :], -jnp.inf).max(axis=(0, 1))
    slot_max = row_max[query_tile]
    exp_terms = jnp.where(live_slot[:, :, None, None], jnp.exp(scores - slot_max[..., None]), 0.0)
    rounded = lax.optimization_barrier(exp_terms.astype(jnp.bfloat16)).astype(jnp.float32)
    value_terms = jnp.einsum("rcij,rcjd->rcid", rounded, value_blocks)
    selector = one_hot.astype(jnp.float32)
    numerator = jnp.einsum("rcq,rcid->rqid", selector, value_terms, precision=lax.Precision.HIGHEST)
    denominator = jnp.einsum("rcq,rci->rqi", selector, exp_terms.sum(-1), precision=lax.Precision.HIGHEST)
    numerator = lax.optimization_barrier(numerator.astype(jnp.bfloat16)).astype(jnp.float32).sum(0)
    denominator = lax.optimization_barrier(denominator.astype(jnp.bfloat16)).astype(jnp.float32).sum(0)
    attention = numerator / denominator[..., None]
    return attention.reshape(Q_LEN, HEAD_DIM).astype(jnp.bfloat16)


def reference(queries, key_states, value_states, block_ids, block_counts, out_weight):
    query_heads = queries.reshape(Q_LEN, HEADS, HEAD_DIM).transpose(1, 0, 2)
    key_heads = key_states.reshape(CTX, HEADS, HEAD_DIM).transpose(1, 0, 2)
    value_heads = value_states.reshape(CTX, HEADS, HEAD_DIM).transpose(1, 0, 2)
    id_table = block_ids.reshape(HEADS, N_KEYS, CAP)
    attention = lax.map(head_attention, (query_heads, key_heads, value_heads, id_table, block_counts))
    flat_rows = attention.transpose(1, 0, 2).reshape(Q_LEN, D)
    return jnp.dot(flat_rows, out_weight, preferred_element_type=jnp.float32).astype(jnp.bfloat16)
```

```python
import functools
import math

import jax
import jax.numpy as jnp
from jax import lax
from jax.experimental import pallas as pl
from jax.experimental.pallas import tpu as pltpu
from jax.sharding import PartitionSpec as P

BLOCK = 128
UNROLL = 16
STAT_ROWS = 16
ABSENT = -3.0e38
F32 = jnp.float32
BF16 = jnp.bfloat16


def split3(x):
    high = x.astype(BF16).astype(F32)
    rest = x - high
    middle = rest.astype(BF16).astype(F32)
    return high, middle, rest - middle


def attend_kernel(ids, counts, q_ref, k_ref, v_ref, out_ref, acc, top, den, stats):
    h = pl.program_id(0)
    head_dim = q_ref.shape[1]
    query_tiles = q_ref.shape[0] // BLOCK
    tiles = k_ref.shape[0] // BLOCK
    scale = head_dim**-0.5 * math.log2(math.e)
    acc[...] = jnp.zeros_like(acc)
    den[...] = jnp.zeros_like(den)
    top[...] = jnp.full_like(top, -jnp.inf)
    count = counts[h, 0]

    def group(step, carry):
        slots = []
        for u in range(UNROLL):
            j = step * UNROLL + u
            live = j < count
            block = jnp.where(live, ids[h, j], 0)
            query = lax.div(block, jnp.int32(tiles))
            tile = lax.rem(block, jnp.int32(tiles))
            slots.append((jnp.where(live, query, query_tiles), query, tile))

        def rows(i):
            return pl.ds(pl.multiple_of(i * BLOCK, BLOCK), BLOCK)

        scores = [
            lax.dot_general(
                k_ref[rows(tile), :],
                q_ref[rows(query), :],
                (((1,), (1,)), ((), ())),
                preferred_element_type=F32,
            )
            for _, query, tile in slots
        ]
        parts = []
        for (slot, _, tile), s in zip(slots, scores):
            s = s * scale
            m = jnp.max(s, axis=0, keepdims=True)
            p = jnp.exp2(s - m)
            d = jnp.sum(p, axis=0, keepdims=True)
            o = lax.dot_general(
                v_ref[rows(tile), :],
                p.astype(BF16),
                (((0,), (0,)), ((), ())),
                preferred_element_type=F32,
            )
            parts.append((slot, m, d, o))
        for slot, m, d, o in parts:
            row = pl.ds(slot, 1)
            old = top[row, :]
            new = jnp.maximum(old, m)
            keep = jnp.exp2(old - new)
            take = jnp.exp2(m - new)
            top[row, :] = new
            den[row, :] = den[row, :] * keep + d * take
            acc[slot] = acc[slot] * keep + o * take
        return carry

    lax.fori_loop(0, (count + UNROLL - 1) // UNROLL, group, 0)

    total = den[0:query_tiles, :]
    listed = total > 0
    safe = jnp.where(listed, total, 1.0)
    level = jnp.where(listed, top[0:query_tiles, :] + jnp.log2(safe), ABSENT)
    den[0:query_tiles, :] = jnp.where(listed, 1.0 / safe, 0.0)
    pieces = split3(level)
    per = out_ref.shape[2] // BLOCK
    heads = pl.num_programs(0)
    for q in range(query_tiles):
        dest, part = divmod(q, per)
        lanes = slice(part * BLOCK, (part + 1) * BLOCK)
        out_ref[dest, pl.ds(pl.multiple_of(h * head_dim, head_dim), head_dim), lanes] = (
            acc[q] * den[q : q + 1, :]
        ).astype(BF16)
        for i, piece in enumerate(pieces):
            stats[dest, h, i : i + 1, lanes] = piece[q : q + 1, :]

    @pl.when(h == heads - 1)
    def _():
        first = out_ref.shape[1] - STAT_ROWS
        heads_here = stats.shape[1]
        rows = [stats[:, i, 0:3, :] for i in range(heads_here)]
        spare = STAT_ROWS - 3 * heads_here
        rows.append(jnp.zeros((stats.shape[0], spare, stats.shape[3]), F32))
        out_ref[:, first:, :] = jnp.concatenate(rows, axis=1).astype(BF16)


def attend(ids, counts, queries, keys, values, ranges):
    heads = ids.shape[0]
    width = queries.shape[1] // heads
    query_tiles = queries.shape[0] // BLOCK
    rows = queries.shape[0] // ranges

    def column(n):
        return pl.BlockSpec((n, width), lambda h, *_: (0, h))

    shape = (ranges, heads * width + STAT_ROWS, rows)
    return pl.pallas_call(
        attend_kernel,
        out_shape=jax.ShapeDtypeStruct(shape, BF16),
        grid_spec=pltpu.PrefetchScalarGridSpec(
            num_scalar_prefetch=2,
            grid=(heads,),
            in_specs=[column(queries.shape[0]), column(keys.shape[0]), column(values.shape[0])],
            out_specs=pl.BlockSpec(shape, lambda h, *_: (0, 0, 0)),
            scratch_shapes=[
                pltpu.VMEM((query_tiles + 1, width, BLOCK), F32),
                pltpu.VMEM((query_tiles + 8, BLOCK), F32),
                pltpu.VMEM((query_tiles + 8, BLOCK), F32),
                pltpu.VMEM((ranges, heads, 8, rows), F32),
            ],
        ),
        compiler_params=pltpu.CompilerParams(
            dimension_semantics=("arbitrary",), vmem_limit_bytes=56 * 1024 * 1024
        ),
        name="attend",
    )(ids, counts, queries, keys, values)


def combine_kernel(heads, in_ref, out_ref):
    ranges, total, rows = in_ref.shape
    width = (total - STAT_ROWS) // heads
    first = total - STAT_ROWS
    stats = in_ref[:, first:, :].astype(F32)
    for h in range(heads):
        level = stats[:, 3 * h, :] + stats[:, 3 * h + 1, :] + stats[:, 3 * h + 2, :]
        level = level - jnp.max(level, axis=0, keepdims=True)
        share = jnp.exp2(level)
        share = share / jnp.sum(share, axis=0, keepdims=True)
        acc = jnp.zeros((width, rows), F32)
        for r in range(ranges):
            acc += in_ref[r, h * width : (h + 1) * width, :].astype(F32) * share[r : r + 1, :]
        out_ref[h * width : (h + 1) * width, :] = acc.astype(BF16)


def combine(parts, heads):
    shape = (parts.shape[1] - STAT_ROWS, parts.shape[2])
    return pl.pallas_call(
        functools.partial(combine_kernel, heads),
        out_shape=jax.ShapeDtypeStruct(shape, BF16),
        compiler_params=pltpu.CompilerParams(vmem_limit_bytes=32 * 1024 * 1024),
        name="combine",
    )(parts)


def local(queries, key_states, value_states, block_ids, block_counts, out_weight):
    heads_here = block_ids.shape[0]
    ranges = lax.axis_size("keys")
    groups = lax.axis_size("heads")
    span = out_weight.shape[1] // groups
    pieces = out_weight.reshape(out_weight.shape[0], groups, span).transpose(1, 0, 2)
    weight = lax.all_to_all(pieces, "heads", split_axis=0, concat_axis=0, tiled=True)
    weight = weight.reshape(out_weight.shape[0] * groups, span)
    every_query = lax.all_gather(queries, "keys", axis=0, tiled=True)
    parts = attend(block_ids, block_counts, every_query, key_states, value_states, ranges)
    got = lax.all_to_all(parts, "keys", split_axis=0, concat_axis=0, tiled=True)
    attention = combine(got, heads_here)
    all_heads = lax.all_gather(attention, "heads", axis=0, tiled=True)
    return lax.dot_general(
        all_heads, weight, (((0,), (0,)), ((), ())), preferred_element_type=F32
    ).astype(BF16)


def solution(mesh):
    in_specs = (
        P("keys", "heads"),
        P("keys", "heads"),
        P("keys", "heads"),
        P("heads", "keys"),
        P("heads", "keys"),
        P("heads", None),
    )
    return jax.shard_map(
        local, mesh=mesh, in_specs=in_specs, out_specs=P("keys", "heads"), check_vma=False
    )
```

```python
import functools
import math

import jax
import jax.numpy as jnp
from jax import lax
from jax.experimental import pallas as pl
from jax.experimental.pallas import tpu as pltpu
from jax.sharding import PartitionSpec as P

BLOCK = 128
UNROLL = 16
STAT_ROWS = 16
ABSENT = -3.0e38
F32 = jnp.float32
BF16 = jnp.bfloat16


def split3(x):
    high = x.astype(BF16).astype(F32)
    rest = x - high
    middle = rest.astype(BF16).astype(F32)
    return high, middle, rest - middle


def attend_kernel(first_head, ids, counts, q_ref, k_ref, v_ref, out_ref, acc, top, den, stats):
    h = pl.program_id(0)
    source = h + first_head
    head_dim = q_ref.shape[1]
    query_tiles = q_ref.shape[0] // BLOCK
    tiles = k_ref.shape[0] // BLOCK
    scale = head_dim**-0.5 * math.log2(math.e)
    acc[...] = jnp.zeros_like(acc)
    den[...] = jnp.zeros_like(den)
    top[...] = jnp.full_like(top, -jnp.inf)
    count = counts[source, 0]

    def group(step, carry):
        slots = []
        for u in range(UNROLL):
            j = step * UNROLL + u
            live = j < count
            block = jnp.where(live, ids[source, j], 0)
            query = lax.div(block, jnp.int32(tiles))
            tile = lax.rem(block, jnp.int32(tiles))
            slots.append((jnp.where(live, query, query_tiles), query, tile))

        def rows(i):
            return pl.ds(pl.multiple_of(i * BLOCK, BLOCK), BLOCK)

        scores = [
            lax.dot_general(
                k_ref[rows(tile), :],
                q_ref[rows(query), :],
                (((1,), (1,)), ((), ())),
                preferred_element_type=F32,
            )
            for _, query, tile in slots
        ]
        parts = []
        for (slot, _, tile), s in zip(slots, scores):
            s = s * scale
            m = jnp.max(s, axis=0, keepdims=True)
            p = jnp.exp2(s - m)
            d = jnp.sum(p, axis=0, keepdims=True)
            o = lax.dot_general(
                v_ref[rows(tile), :],
                p.astype(BF16),
                (((0,), (0,)), ((), ())),
                preferred_element_type=F32,
            )
            parts.append((slot, m, d, o))
        for slot, m, d, o in parts:
            row = pl.ds(slot, 1)
            old = top[row, :]
            new = jnp.maximum(old, m)
            keep = jnp.exp2(old - new)
            take = jnp.exp2(m - new)
            top[row, :] = new
            den[row, :] = den[row, :] * keep + d * take
            acc[slot] = acc[slot] * keep + o * take
        return carry

    lax.fori_loop(0, (count + UNROLL - 1) // UNROLL, group, 0)

    total = den[0:query_tiles, :]
    listed = total > 0
    safe = jnp.where(listed, total, 1.0)
    level = jnp.where(listed, top[0:query_tiles, :] + jnp.log2(safe), ABSENT)
    den[0:query_tiles, :] = jnp.where(listed, 1.0 / safe, 0.0)
    pieces = split3(level)
    per = out_ref.shape[2] // BLOCK
    heads = pl.num_programs(0)
    for q in range(query_tiles):
        dest, part = divmod(q, per)
        lanes = slice(part * BLOCK, (part + 1) * BLOCK)
        out_ref[dest, pl.ds(pl.multiple_of(h * head_dim, head_dim), head_dim), lanes] = (
            acc[q] * den[q : q + 1, :]
        ).astype(BF16)
        for i, piece in enumerate(pieces):
            stats[dest, h, i : i + 1, lanes] = piece[q : q + 1, :]

    @pl.when(h == heads - 1)
    def _():
        first = out_ref.shape[1] - STAT_ROWS
        heads_here = stats.shape[1]
        rows = [stats[:, i, 0:3, :] for i in range(heads_here)]
        spare = STAT_ROWS - 3 * heads_here
        rows.append(jnp.zeros((stats.shape[0], spare, stats.shape[3]), F32))
        out_ref[:, first:, :] = jnp.concatenate(rows, axis=1).astype(BF16)


def attend(ids, counts, queries, keys, values, ranges, first_head, heads):
    width = queries.shape[1] // ids.shape[0]
    query_tiles = queries.shape[0] // BLOCK
    rows = queries.shape[0] // ranges

    def column(n):
        return pl.BlockSpec((n, width), lambda h, *_: (0, h + first_head))

    shape = (ranges, heads * width + STAT_ROWS, rows)
    return pl.pallas_call(
        functools.partial(attend_kernel, first_head),
        out_shape=jax.ShapeDtypeStruct(shape, BF16),
        grid_spec=pltpu.PrefetchScalarGridSpec(
            num_scalar_prefetch=2,
            grid=(heads,),
            in_specs=[column(queries.shape[0]), column(keys.shape[0]), column(values.shape[0])],
            out_specs=pl.BlockSpec(shape, lambda h, *_: (0, 0, 0)),
            scratch_shapes=[
                pltpu.VMEM((query_tiles + 1, width, BLOCK), F32),
                pltpu.VMEM((query_tiles + 8, BLOCK), F32),
                pltpu.VMEM((query_tiles + 8, BLOCK), F32),
                pltpu.VMEM((ranges, heads, 8, rows), F32),
            ],
        ),
        compiler_params=pltpu.CompilerParams(
            dimension_semantics=("arbitrary",), vmem_limit_bytes=56 * 1024 * 1024
        ),
        name="attend",
    )(ids, counts, queries, keys, values)


def combine_kernel(heads, in_ref, out_ref):
    ranges, total, rows = in_ref.shape
    width = (total - STAT_ROWS) // heads
    first = total - STAT_ROWS
    stats = in_ref[:, first:, :].astype(F32)
    for h in range(heads):
        level = stats[:, 3 * h, :] + stats[:, 3 * h + 1, :] + stats[:, 3 * h + 2, :]
        level = level - jnp.max(level, axis=0, keepdims=True)
        share = jnp.exp2(level)
        share = share / jnp.sum(share, axis=0, keepdims=True)
        acc = jnp.zeros((width, rows), F32)
        for r in range(ranges):
            acc += in_ref[r, h * width : (h + 1) * width, :].astype(F32) * share[r : r + 1, :]
        out_ref[h * width : (h + 1) * width, :] = acc.astype(BF16)


def combine(parts, heads):
    shape = (parts.shape[1] - STAT_ROWS, parts.shape[2])
    return pl.pallas_call(
        functools.partial(combine_kernel, heads),
        out_shape=jax.ShapeDtypeStruct(shape, BF16),
        compiler_params=pltpu.CompilerParams(vmem_limit_bytes=32 * 1024 * 1024),
        name="combine",
    )(parts)


def gather_heads(x):
    groups = lax.axis_size("heads")
    pieces = [x]
    for d in GROUP_STEPS[1:]:
        pairs = [(g, (g + 2 * d) % groups) for g in range(groups)]
        pieces.append(lax.ppermute(x, "heads", pairs))
    same = jnp.stack(pieces)
    other = lax.ppermute(same, "heads", [(g, g ^ 1) for g in range(groups)])
    return same, other


GROUP_STEPS = (0, 1, 3, 2)


def local(queries, key_states, value_states, block_ids, block_counts, out_weight):
    heads_here = block_ids.shape[0]
    ranges = lax.axis_size("keys")
    groups = lax.axis_size("heads")
    me = lax.axis_index("heads")
    span = out_weight.shape[1] // groups
    half = heads_here // 2
    cut = out_weight.shape[0] // 2

    def exchange(parts):
        return lax.all_to_all(parts, "keys", split_axis=0, concat_axis=0, tiled=True)

    def attend_half(first):
        return attend(
            block_ids, block_counts, every_query, key_states, value_states, ranges, first, half
        )

    def project(rows, weights):
        return lax.dot_general(
            rows, weights, (((0, 1), (0, 1)), ((), ())), preferred_element_type=F32
        )

    every_query = lax.all_gather(queries, "keys", axis=0, tiled=True)
    pieces = out_weight.reshape(out_weight.shape[0], groups, span).transpose(1, 0, 2)
    weight = lax.all_to_all(pieces, "heads", split_axis=0, concat_axis=0, tiled=True)

    early = attend_half(0)
    early, weight = lax.optimization_barrier((early, weight))
    early_got = exchange(early)
    late = attend_half(half)
    order = [jnp.bitwise_xor((me - 2 * d) % groups, c) for c in (0, 1) for d in GROUP_STEPS]
    late_weight = [
        lax.dynamic_slice(weight, (g, cut, 0), (1, cut, span)) for g in order
    ]
    late_weight = jnp.concatenate(late_weight)
    early_weight = weight[:, :cut]
    late, late_weight, early_weight = lax.optimization_barrier((late, late_weight, early_weight))
    late_got = exchange(late)
    early_rows = combine(early_got, half)
    early_all = lax.all_gather(early_rows, "heads", axis=0)
    total = project(early_all, early_weight)
    same, other = gather_heads(combine(late_got, half))
    total += project(same, late_weight[: groups // 2])
    total += project(other, late_weight[groups // 2 :])
    return total.astype(BF16)


def solution(mesh):
    in_specs = (
        P("keys", "heads"),
        P("keys", "heads"),
        P("keys", "heads"),
        P("heads", "keys"),
        P("heads", "keys"),
        P("heads", None),
    )
    return jax.shard_map(
        local, mesh=mesh, in_specs=in_specs, out_specs=P("keys", "heads"), check_vma=False
    )
```

```python
import functools
import math

import jax
import jax.numpy as jnp
from jax import lax
from jax.experimental import pallas as pl
from jax.experimental.pallas import tpu as pltpu
from jax.sharding import PartitionSpec as P

BLOCK = 128
UNROLL = 16
STAT_ROWS = 16
ABSENT = -3.0e38
Z_STEPS = (1, 3, 2)
F32 = jnp.float32
BF16 = jnp.bfloat16


def split3(x):
    high = x.astype(BF16).astype(F32)
    rest = x - high
    middle = rest.astype(BF16).astype(F32)
    return high, middle, rest - middle


def plan_kernel(tiles, owned, ids, counts, entries, starts):
    heads = ids.shape[0]
    zero = jnp.int32(0)

    def over_head(h, at):
        for c in range(owned):
            starts[c, h] = at[c]

        def one(j, at):
            block = ids[h, j]
            query = lax.div(block, jnp.int32(tiles))
            tile = lax.rem(block, jnp.int32(tiles))
            chunk = lax.rem(query, jnp.int32(owned))
            owner = lax.div(query, jnp.int32(owned))
            place = at[0]
            for c in range(1, owned):
                place = jnp.where(chunk == c, at[c], place)
            entries[chunk, place] = (h * 256 + owner) * 256 + tile
            return tuple(a + jnp.where(chunk == c, 1, 0) for c, a in enumerate(at))

        return lax.fori_loop(0, counts[h, 0], one, at)

    at = lax.fori_loop(0, heads, over_head, (zero,) * owned)
    for c in range(owned):
        starts[c, heads] = at[c]


def plan(ids, counts, tiles, owned):
    heads, slots = ids.shape
    smem = pl.BlockSpec(memory_space=pltpu.SMEM)
    return pl.pallas_call(
        functools.partial(plan_kernel, tiles, owned),
        out_shape=(
            jax.ShapeDtypeStruct((owned, heads * slots), jnp.int32),
            jax.ShapeDtypeStruct((owned, heads + 1), jnp.int32),
        ),
        in_specs=[smem, smem],
        out_specs=(smem, smem),
        name="plan",
    )(ids, counts)


def attend_kernel(
    chunk, entries, starts, q_hbm, k_hbm, v_hbm, out_ref, qs, ks, vs, acc, top, den, stats, sems
):
    heads, _, width = ks.shape
    owners = qs.shape[1] // BLOCK
    scale = width**-0.5 * math.log2(math.e)

    def copies(h):
        lanes = pl.ds(h * width, width)
        return [
            pltpu.make_async_copy(src.at[:, lanes], dst.at[h], sems.at[h, i])
            for i, (src, dst) in enumerate(((q_hbm, qs), (k_hbm, ks), (v_hbm, vs)))
        ]

    for h in range(heads):
        for copy in copies(h):
            copy.start()
    acc[...] = jnp.zeros_like(acc)
    den[...] = jnp.zeros_like(den)
    top[...] = jnp.full_like(top, -jnp.inf)
    count = starts[chunk, heads]
    groups = lax.div(count + UNROLL - 1, jnp.int32(UNROLL))
    opens = [lax.div(starts[chunk, h], jnp.int32(UNROLL)) for h in range(heads)]

    def group(step, carry):
        for h in range(heads):

            @pl.when(step == opens[h])
            def _():
                for copy in copies(h):
                    copy.wait()

        slots = []
        for u in range(UNROLL):
            j = step * UNROLL + u
            live = j < count
            entry = jnp.where(live, entries[chunk, j], 0)
            head = lax.shift_right_logical(entry, 16)
            owner = lax.bitwise_and(lax.shift_right_logical(entry, 8), 255)
            tile = lax.bitwise_and(entry, 255)
            slots.append((jnp.where(live, head * owners + owner, heads * owners), head, owner, tile))

        def rows(i):
            return pl.ds(pl.multiple_of(i * BLOCK, BLOCK), BLOCK)

        scores = [
            lax.dot_general(
                ks[head, rows(tile), :],
                qs[head, rows(owner), :],
                (((1,), (1,)), ((), ())),
                preferred_element_type=F32,
            )
            for _, head, owner, tile in slots
        ]
        parts = []
        for (slot, head, _, tile), s in zip(slots, scores):
            s = s * scale
            m = jnp.max(s, axis=0, keepdims=True)
            p = jnp.exp2(s - m)
            d = jnp.sum(p, axis=0, keepdims=True)
            o = lax.dot_general(
                vs[head, rows(tile), :],
                p.astype(BF16),
                (((0,), (0,)), ((), ())),
                preferred_element_type=F32,
            )
            parts.append((slot, m, d, o))
        for slot, m, d, o in parts:
            row = pl.ds(slot, 1)
            old = top[row, :]
            new = jnp.maximum(old, m)
            keep = jnp.exp2(old - new)
            take = jnp.exp2(m - new)
            top[row, :] = new
            den[row, :] = den[row, :] * keep + d * take
            acc[slot] = acc[slot] * keep + o * take
        return carry

    lax.fori_loop(0, groups, group, 0)
    for h in range(heads):

        @pl.when(opens[h] >= groups)
        def _():
            for copy in copies(h):
                copy.wait()

    used = heads * owners
    total = den[0:used, :]
    listed = total > 0
    safe = jnp.where(listed, total, 1.0)
    level = jnp.where(listed, top[0:used, :] + jnp.log2(safe), ABSENT)
    den[0:used, :] = jnp.where(listed, 1.0 / safe, 0.0)
    for h in range(heads):
        for q in range(owners):
            at = h * owners + q
            out_ref[q, h * width : (h + 1) * width, :] = (acc[at] * den[at : at + 1, :]).astype(BF16)
        for i, piece in enumerate(split3(level[h * owners : (h + 1) * owners])):
            stats[3 * h + i] = piece
    first = out_ref.shape[1] - STAT_ROWS
    for q in range(owners):
        rows = [stats[i, q : q + 1, :] for i in range(3 * heads)]
        rows.append(jnp.zeros((STAT_ROWS - 3 * heads, BLOCK), F32))
        out_ref[q, first:, :] = jnp.concatenate(rows, axis=0).astype(BF16)


def attend(chunk, entries, starts, queries, keys, values, heads):
    width = queries.shape[1] // heads
    owners = queries.shape[0] // BLOCK
    smem = pl.BlockSpec(memory_space=pltpu.SMEM)
    hbm = pl.BlockSpec(memory_space=pltpu.HBM)
    lines = -(-(heads * owners + 1) // 8) * 8
    return pl.pallas_call(
        functools.partial(attend_kernel, chunk),
        out_shape=jax.ShapeDtypeStruct((owners, heads * width + STAT_ROWS, BLOCK), BF16),
        in_specs=[smem, smem, hbm, hbm, hbm],
        scratch_shapes=[
            pltpu.VMEM((heads, queries.shape[0], width), BF16),
            pltpu.VMEM((heads, keys.shape[0], width), BF16),
            pltpu.VMEM((heads, values.shape[0], width), BF16),
            pltpu.VMEM((heads * owners + 1, width, BLOCK), F32),
            pltpu.VMEM((lines, BLOCK), F32),
            pltpu.VMEM((lines, BLOCK), F32),
            pltpu.VMEM((3 * heads, owners, BLOCK), F32),
            pltpu.SemaphoreType.DMA((heads, 3)),
        ],
        compiler_params=pltpu.CompilerParams(vmem_limit_bytes=48 * 1024 * 1024),
        name="attend",
    )(entries, starts, queries, keys, values)


def project_kernel(heads, core, in_ref, own_weight, other_weight, own_ref, other_ref, mixed):
    ranges, total, rows = in_ref.shape
    width = (total - STAT_ROWS) // heads
    first = total - STAT_ROWS

    @pl.when(pl.program_id(0) == 0)
    def _():
        stats = in_ref[:, first:, :].astype(F32)
        for h in range(heads):
            level = stats[:, 3 * h, :] + stats[:, 3 * h + 1, :] + stats[:, 3 * h + 2, :]
            share = jnp.exp2(level - jnp.max(level, axis=0, keepdims=True))
            share = share / jnp.sum(share, axis=0, keepdims=True)
            acc = jnp.zeros((width, rows), F32)
            for r in range(ranges):
                acc += in_ref[r, h * width : (h + 1) * width, :].astype(F32) * share[r : r + 1, :]
            mixed[h * width : (h + 1) * width, :] = acc.astype(BF16)

    for weight, out_ref in ((own_weight, own_ref), (other_weight, other_ref)):
        out_ref[0] = lax.dot_general(
            mixed[...], weight[...], (((0,), (0,)), ((), ())), preferred_element_type=F32
        ).astype(BF16)


def project(core, parts, weight, heads, span):
    depth = weight.shape[0]
    zs = weight.shape[1] // span // 2
    rows = parts.shape[2]
    result = pl.BlockSpec((1, rows, span), lambda z, core: (z, 0, 0))
    return pl.pallas_call(
        functools.partial(project_kernel, heads),
        out_shape=[jax.ShapeDtypeStruct((zs, rows, span), BF16)] * 2,
        grid_spec=pltpu.PrefetchScalarGridSpec(
            num_scalar_prefetch=1,
            grid=(zs,),
            in_specs=[
                pl.BlockSpec(parts.shape, lambda z, core: (0, 0, 0)),
                pl.BlockSpec((depth, span), lambda z, core: (0, 2 * z + core[0])),
                pl.BlockSpec((depth, span), lambda z, core: (0, 2 * z + 1 - core[0])),
            ],
            out_specs=[result, result],
            scratch_shapes=[pltpu.VMEM((depth, rows), BF16)],
        ),
        compiler_params=pltpu.CompilerParams(
            dimension_semantics=("arbitrary",), vmem_limit_bytes=32 * 1024 * 1024
        ),
        name="project",
    )(core, parts, weight, weight)


def pair_kernel(z, mine, theirs, own, *others):
    zs = mine.shape[0]
    for d, out in zip((0,) + Z_STEPS, (own,) + others):
        at = lax.rem(z[0] + d, jnp.int32(zs))
        out[...] = (mine[at].astype(F32) + theirs[at].astype(F32)).astype(out.dtype)


def pair(z, mine, theirs):
    shape = mine.shape[1:]
    vmem = pl.BlockSpec(memory_space=pltpu.VMEM)
    return pl.pallas_call(
        pair_kernel,
        out_shape=[jax.ShapeDtypeStruct(shape, F32)]
        + [jax.ShapeDtypeStruct(shape, BF16) for _ in Z_STEPS],
        in_specs=[pl.BlockSpec(memory_space=pltpu.SMEM), vmem, vmem],
        name="pair",
    )(z, mine, theirs)


def local(queries, key_states, value_states, block_ids, block_counts, out_weight):
    heads = block_ids.shape[0]
    ranges = lax.axis_size("keys")
    groups = lax.axis_size("heads")
    me = lax.axis_index("heads")
    core = jnp.reshape(me % 2, (1,)).astype(jnp.int32)
    z = jnp.reshape(me // 2, (1,)).astype(jnp.int32)
    span = out_weight.shape[1] // groups
    tiles = key_states.shape[0] // BLOCK
    owned = queries.shape[0] // BLOCK

    def exchange(parts):
        return lax.all_to_all(parts, "keys", split_axis=0, concat_axis=0, tiled=True)

    def finish(got):
        mine, theirs = project(core, got, out_weight, heads, span)
        swap = [(g, g ^ 1) for g in range(groups)]
        own, *others = pair(z, mine, lax.ppermute(theirs, "heads", swap))
        total = own
        for d, piece in zip(Z_STEPS, others):
            pairs = [(g, (g + 2 * d) % groups) for g in range(groups)]
            total = total + lax.ppermute(piece, "heads", pairs).astype(F32)
        return total.astype(BF16)

    def rows(c):
        return queries[c * BLOCK : (c + 1) * BLOCK]

    copies = jnp.broadcast_to(rows(0)[None], (ranges,) + rows(0).shape)
    first = exchange(copies).reshape(ranges * BLOCK, queries.shape[1])
    gathered = [first] + [
        lax.all_gather(rows(c), "keys", axis=0, tiled=True) for c in range(1, owned)
    ]
    entries, starts = plan(block_ids, block_counts, tiles, owned)
    outs = []
    for c in range(owned):
        parts = attend(c, entries, starts, gathered[c], key_states, value_states, heads)
        got = exchange(parts)
        if outs:
            got, outs[-1] = lax.optimization_barrier((got, outs[-1]))
        outs.append(finish(got))
    return jnp.concatenate(outs)


def solution(mesh):
    in_specs = (
        P("keys", "heads"),
        P("keys", "heads"),
        P("keys", "heads"),
        P("heads", "keys"),
        P("heads", "keys"),
        P("heads", None),
    )
    return jax.shard_map(
        local, mesh=mesh, in_specs=in_specs, out_specs=P("keys", "heads"), check_vma=False
    )
```

```python
import functools
import math

import jax
import jax.numpy as jnp
from jax import lax
from jax.experimental import pallas as pl
from jax.experimental.pallas import tpu as pltpu
from jax.sharding import PartitionSpec as P

BLOCK = 128
UNROLL = 16
STAT_ROWS = 16
ABSENT = -3.0e38
Z_STEPS = (1, 3, 2)
F32 = jnp.float32
BF16 = jnp.bfloat16


def split3(x):
    high = x.astype(BF16).astype(F32)
    rest = x - high
    middle = rest.astype(BF16).astype(F32)
    return high, middle, rest - middle


def plan_kernel(tiles, owned, side, me, ids, counts, entries, starts):
    heads = ids.shape[0]
    my_x = lax.div(me[0], jnp.int32(side))
    my_y = lax.rem(me[0], jnp.int32(side))
    zero = jnp.int32(0)

    def over_head(h, at):
        for c in range(owned):
            starts[c, h] = at[c]

        def one(j, at):
            block = ids[h, j]
            query = lax.div(block, jnp.int32(tiles))
            tile = lax.rem(block, jnp.int32(tiles))
            chunk = lax.rem(query, jnp.int32(owned))
            owner = lax.div(query, jnp.int32(owned))
            dx = lax.rem(my_x - lax.div(owner, jnp.int32(side)) + side, jnp.int32(side))
            dy = lax.rem(my_y - lax.rem(owner, jnp.int32(side)) + side, jnp.int32(side))
            near = jnp.where(h < heads // 2, dy * side + dx, dx * side + dy)
            position = jnp.where(chunk == 0, near, owner)
            place = at[0]
            for c in range(1, owned):
                place = jnp.where(chunk == c, at[c], place)
            entries[chunk, place] = ((h * 256 + owner) * 256 + position) * 256 + tile
            return tuple(a + jnp.where(chunk == c, 1, 0) for c, a in enumerate(at))

        return lax.fori_loop(0, counts[h, 0], one, at)

    at = lax.fori_loop(0, heads, over_head, (zero,) * owned)
    for c in range(owned):
        starts[c, heads] = at[c]


def plan(me, ids, counts, tiles, owned, side):
    heads, slots = ids.shape
    smem = pl.BlockSpec(memory_space=pltpu.SMEM)
    return pl.pallas_call(
        functools.partial(plan_kernel, tiles, owned, side),
        out_shape=(
            jax.ShapeDtypeStruct((owned, heads * slots), jnp.int32),
            jax.ShapeDtypeStruct((owned, heads + 1), jnp.int32),
        ),
        in_specs=[smem, smem, smem],
        out_specs=(smem, smem),
        compiler_params=pltpu.CompilerParams(vmem_limit_bytes=1024 * 1024),
        name="plan",
    )(me, ids, counts)


def attend_kernel(chunk, sources, entries, starts, *refs):
    blocks = 1 + max(i for pieces in sources for i, _ in pieces)
    q_hbm = refs[:blocks]
    k_hbm, v_hbm, out_ref, qs, ks, vs, acc, top, den, stats, sems = refs[blocks:]
    heads, _, width = ks.shape
    owners = qs.shape[1] // BLOCK
    scale = width**-0.5 * math.log2(math.e)

    def copies(h):
        moves = [(k_hbm.at[:, h * width : (h + 1) * width], ks.at[h])]
        moves.append((v_hbm.at[:, h * width : (h + 1) * width], vs.at[h]))
        for n, (i, lane) in enumerate(sources[h]):
            rows = q_hbm[i].shape[0]
            src = q_hbm[i].at[:, lane * width : (lane + 1) * width]
            moves.append((src, qs.at[h, n * rows : (n + 1) * rows]))
        return [
            pltpu.make_async_copy(src, dst, sems.at[h, i]) for i, (src, dst) in enumerate(moves)
        ]

    for h in range(heads):
        for copy in copies(h):
            copy.start()
    acc[...] = jnp.zeros_like(acc)
    den[...] = jnp.zeros_like(den)
    top[...] = jnp.full_like(top, -jnp.inf)
    count = starts[chunk, heads]
    groups = lax.div(count + UNROLL - 1, jnp.int32(UNROLL))
    opens = [lax.div(starts[chunk, h], jnp.int32(UNROLL)) for h in range(heads)]

    def group(step, carry):
        for h in range(heads):

            @pl.when(step == opens[h])
            def _():
                for copy in copies(h):
                    copy.wait()

        slots = []
        for u in range(UNROLL):
            j = step * UNROLL + u
            live = j < count
            entry = jnp.where(live, entries[chunk, j], 0)
            head = lax.shift_right_logical(entry, 24)
            owner = lax.bitwise_and(lax.shift_right_logical(entry, 16), 255)
            position = lax.bitwise_and(lax.shift_right_logical(entry, 8), 255)
            tile = lax.bitwise_and(entry, 255)
            slot = jnp.where(live, head * owners + owner, heads * owners)
            slots.append((slot, head, position, tile))

        def rows(i):
            return pl.ds(pl.multiple_of(i * BLOCK, BLOCK), BLOCK)

        scores = [
            lax.dot_general(
                ks[head, rows(tile), :],
                qs[head, rows(position), :],
                (((1,), (1,)), ((), ())),
                preferred_element_type=F32,
            )
            for _, head, position, tile in slots
        ]
        parts = []
        for (slot, head, _, tile), s in zip(slots, scores):
            s = s * scale
            m = jnp.max(s, axis=0, keepdims=True)
            p = jnp.exp2(s - m)
            d = jnp.sum(p, axis=0, keepdims=True)
            o = lax.dot_general(
                vs[head, rows(tile), :],
                p.astype(BF16),
                (((0,), (0,)), ((), ())),
                preferred_element_type=F32,
            )
            parts.append((slot, m, d, o))
        for slot, m, d, o in parts:
            row = pl.ds(slot, 1)
            old = top[row, :]
            new = jnp.maximum(old, m)
            keep = jnp.exp2(old - new)
            take = jnp.exp2(m - new)
            top[row, :] = new
            den[row, :] = den[row, :] * keep + d * take
            acc[slot] = acc[slot] * keep + o * take
        return carry

    lax.fori_loop(0, groups, group, 0)
    for h in range(heads):

        @pl.when(opens[h] >= groups)
        def _():
            for copy in copies(h):
                copy.wait()

    used = heads * owners
    total = den[0:used, :]
    listed = total > 0
    safe = jnp.where(listed, total, 1.0)
    level = jnp.where(listed, top[0:used, :] + jnp.log2(safe), ABSENT)
    den[0:used, :] = jnp.where(listed, 1.0 / safe, 0.0)
    for h in range(heads):
        for q in range(owners):
            at = h * owners + q
            out_ref[q, h * width : (h + 1) * width, :] = (acc[at] * den[at : at + 1, :]).astype(BF16)
        for i, piece in enumerate(split3(level[h * owners : (h + 1) * owners])):
            stats[3 * h + i] = piece
    first = out_ref.shape[1] - STAT_ROWS
    for q in range(owners):
        rows = [stats[i, q : q + 1, :] for i in range(3 * heads)]
        rows.append(jnp.zeros((STAT_ROWS - 3 * heads, BLOCK), F32))
        out_ref[q, first:, :] = jnp.concatenate(rows, axis=0).astype(BF16)


def in_hbm(x):
    return pltpu.with_memory_space_constraint(x, pltpu.HBM)


def attend(chunk, entries, starts, queries, sources, keys, values):
    heads = len(sources)
    width = keys.shape[1] // heads
    count = sum(queries[i].shape[0] for i, _ in sources[0])
    owners = count // BLOCK
    smem = pl.BlockSpec(memory_space=pltpu.SMEM)
    hbm = pl.BlockSpec(memory_space=pl.ANY)
    lines = -(-(heads * owners + 1) // 8) * 8
    return pl.pallas_call(
        functools.partial(attend_kernel, chunk, sources),
        out_shape=jax.ShapeDtypeStruct((owners, heads * width + STAT_ROWS, BLOCK), BF16),
        in_specs=[smem, smem] + [hbm] * (len(queries) + 2),
        scratch_shapes=[
            pltpu.VMEM((heads, count, width), BF16),
            pltpu.VMEM((heads, keys.shape[0], width), BF16),
            pltpu.VMEM((heads, values.shape[0], width), BF16),
            pltpu.VMEM((heads * owners + 1, width, BLOCK), F32),
            pltpu.VMEM((lines, BLOCK), F32),
            pltpu.VMEM((lines, BLOCK), F32),
            pltpu.VMEM((3 * heads, owners, BLOCK), F32),
            pltpu.SemaphoreType.DMA((heads, 2 + max(len(p) for p in sources))),
        ],
        compiler_params=pltpu.CompilerParams(vmem_limit_bytes=48 * 1024 * 1024),
        name="attend",
    )(entries, starts, *queries, in_hbm(keys), in_hbm(values))


def project_kernel(heads, core, in_ref, own_weight, other_weight, own_ref, other_ref, mixed):
    ranges, total, rows = in_ref.shape
    width = (total - STAT_ROWS) // heads
    first = total - STAT_ROWS

    @pl.when(pl.program_id(0) == 0)
    def _():
        stats = in_ref[:, first:, :].astype(F32)
        for h in range(heads):
            level = stats[:, 3 * h, :] + stats[:, 3 * h + 1, :] + stats[:, 3 * h + 2, :]
            share = jnp.exp2(level - jnp.max(level, axis=0, keepdims=True))
            share = share / jnp.sum(share, axis=0, keepdims=True)
            acc = jnp.zeros((width, rows), F32)
            for r in range(ranges):
                acc += in_ref[r, h * width : (h + 1) * width, :].astype(F32) * share[r : r + 1, :]
            mixed[h * width : (h + 1) * width, :] = acc.astype(BF16)

    for weight, out_ref in ((own_weight, own_ref), (other_weight, other_ref)):
        out_ref[0] = lax.dot_general(
            mixed[...], weight[...], (((0,), (0,)), ((), ())), preferred_element_type=F32
        ).astype(BF16)


def project(core, parts, weight, heads, span):
    depth = weight.shape[0]
    zs = weight.shape[1] // span // 2
    rows = parts.shape[2]
    result = pl.BlockSpec((1, rows, span), lambda z, core: (z, 0, 0))
    return pl.pallas_call(
        functools.partial(project_kernel, heads),
        out_shape=[jax.ShapeDtypeStruct((zs, rows, span), BF16)] * 2,
        grid_spec=pltpu.PrefetchScalarGridSpec(
            num_scalar_prefetch=1,
            grid=(zs,),
            in_specs=[
                pl.BlockSpec(parts.shape, lambda z, core: (0, 0, 0)),
                pl.BlockSpec((depth, span), lambda z, core: (0, 2 * z + core[0])),
                pl.BlockSpec((depth, span), lambda z, core: (0, 2 * z + 1 - core[0])),
            ],
            out_specs=[result, result],
            scratch_shapes=[pltpu.VMEM((depth, rows), BF16)],
        ),
        compiler_params=pltpu.CompilerParams(
            dimension_semantics=("arbitrary",), vmem_limit_bytes=32 * 1024 * 1024
        ),
        name="project",
    )(core, parts, in_hbm(weight), in_hbm(weight))


def pair_kernel(z, mine, theirs, own, *others):
    zs = mine.shape[0]
    for d, out in zip((0,) + Z_STEPS, (own,) + others):
        at = lax.rem(z[0] + d, jnp.int32(zs))
        out[...] = (mine[at].astype(F32) + theirs[at].astype(F32)).astype(out.dtype)


def pair(z, mine, theirs):
    shape = mine.shape[1:]
    whole = pl.BlockSpec(mine.shape, lambda i, z: (0, 0, 0))
    return pl.pallas_call(
        pair_kernel,
        out_shape=[jax.ShapeDtypeStruct(shape, F32)]
        + [jax.ShapeDtypeStruct(shape, BF16) for _ in Z_STEPS],
        grid_spec=pltpu.PrefetchScalarGridSpec(
            num_scalar_prefetch=1,
            grid=(1,),
            in_specs=[whole, whole],
            out_specs=[pl.BlockSpec(shape, lambda i, z: (0, 0))] * (1 + len(Z_STEPS)),
        ),
        compiler_params=pltpu.CompilerParams(vmem_limit_bytes=8 * 1024 * 1024),
        name="pair",
    )(z, mine, theirs)


def local(queries, key_states, value_states, block_ids, block_counts, out_weight):
    heads = block_ids.shape[0]
    ranges = lax.axis_size("keys")
    groups = lax.axis_size("heads")
    me = lax.axis_index("heads")
    core = jnp.reshape(me % 2, (1,)).astype(jnp.int32)
    z = jnp.reshape(me // 2, (1,)).astype(jnp.int32)
    span = out_weight.shape[1] // groups
    tiles = key_states.shape[0] // BLOCK
    owned = queries.shape[0] // BLOCK
    side = math.isqrt(ranges)

    def exchange(parts):
        return lax.all_to_all(parts, "keys", split_axis=0, concat_axis=0, tiled=True)

    def finish(got):
        mine, theirs = project(core, got, out_weight, heads, span)
        swap = [(g, g ^ 1) for g in range(groups)]
        own, *others = pair(z, mine, lax.ppermute(theirs, "heads", swap))
        total = own
        for d, piece in zip(Z_STEPS, others):
            pairs = [(g, (g + 2 * d) % groups) for g in range(groups)]
            total = total + lax.ppermute(piece, "heads", pairs).astype(F32)
        return total.astype(BF16)

    def rows(c):
        return queries[c * BLOCK : (c + 1) * BLOCK]

    def along(x, axis):
        def pairs(d):
            there = lambda i, j: ((i + d) % side, j) if axis == 0 else (i, (j + d) % side)
            moved = [there(k // side, k % side) for k in range(ranges)]
            return [(k, i * side + j) for k, (i, j) in enumerate(moved)]

        got = {d: lax.ppermute(x, "keys", pairs(d)) for d in Z_STEPS}
        return [x] + [got[d] for d in range(1, side)]

    near = rows(0)
    middle = near.shape[1] // 2
    left, right = near[:, :middle], near[:, middle:]
    left, right = lax.optimization_barrier((left, right))
    halves = along(left, 0) + along(right, 1)
    halves = lax.optimization_barrier(halves)
    left, right = jnp.concatenate(halves[:side]), jnp.concatenate(halves[side:])
    left, right = lax.optimization_barrier((left, right))
    direct = lax.optimization_barrier(along(left, 1) + along(right, 0))
    lower = [[(i, h) for i in range(side)] for h in range(heads // 2)]
    upper = [[(side + i, h) for i in range(side)] for h in range(heads // 2)]
    whole = [[(0, h)] for h in range(heads)]

    slot = jnp.reshape(lax.axis_index("keys"), (1,)).astype(jnp.int32)
    entries, starts = plan(slot, block_ids, block_counts, tiles, owned, side)
    outs = []
    for c in range(owned):
        if c == 0:
            source, lanes = direct, lower + upper
        else:
            source, lanes = [in_hbm(lax.all_gather(rows(c), "keys", axis=0, tiled=True))], whole
        parts = attend(c, entries, starts, source, lanes, key_states, value_states)
        got = exchange(parts)
        if outs:
            got, outs[-1] = lax.optimization_barrier((got, outs[-1]))
        outs.append(finish(got))
    return jnp.concatenate(outs)


def solution(mesh):
    in_specs = (
        P("keys", "heads"),
        P("keys", "heads"),
        P("keys", "heads"),
        P("heads", "keys"),
        P("heads", "keys"),
        P("heads", None),
    )
    return jax.shard_map(
        local, mesh=mesh, in_specs=in_specs, out_specs=P("keys", "heads"), check_vma=False
    )
```

```python
import functools
import math

import jax
import jax.numpy as jnp
from jax import lax
from jax.experimental import pallas as pl
from jax.experimental.pallas import tpu as pltpu
from jax.sharding import PartitionSpec as P

BLOCK = 128
UNROLL = 16
PLAN_UNROLL = 8
CHUNK_BIT = 28
STAT_ROWS = 16
ABSENT = -3.0e38
Z_STEPS = (1, 3, 2)
F32 = jnp.float32
BF16 = jnp.bfloat16


def split3(x):
    high = x.astype(BF16).astype(F32)
    rest = x - high
    middle = rest.astype(BF16).astype(F32)
    return high, middle, rest - middle


def plan_kernel(owned, codes, counts, entries, starts):
    heads = codes.shape[0]

    def over_head(h, at):
        for c in range(owned):
            starts[c, h] = at[c]
        count = counts[h, 0]

        def some(step, at):
            for u in range(PLAN_UNROLL):
                j = step * PLAN_UNROLL + u
                code = codes[h, j]
                chunk = lax.shift_right_logical(code, CHUNK_BIT)
                place = at[0]
                for c in range(1, owned):
                    place = jnp.where(chunk == c, at[c], place)
                entries[chunk, place] = code
                live = j < count
                at = tuple(
                    a + jnp.where(live & (chunk == c), 1, 0) for c, a in enumerate(at)
                )
            return at

        return lax.fori_loop(0, lax.div(count + PLAN_UNROLL - 1, PLAN_UNROLL), some, at)

    at = lax.fori_loop(0, heads, over_head, (jnp.int32(0),) * owned)
    for c in range(owned):
        starts[c, heads] = at[c]


def plan(me, ids, counts, tiles, owned, side):
    heads, slots = ids.shape
    query, tile = ids // tiles, ids % tiles
    owner, chunk = query // owned, query % owned
    dx = (me // side - owner // side) % side
    dy = (me % side - owner % side) % side
    head = jnp.arange(heads, dtype=jnp.int32)[:, None]
    near = jnp.where(head < heads // 2, dy * side + dx, dx * side + dy)
    position = jnp.where(chunk == 0, near, owner)
    codes = (((chunk * 16 + head) * 256 + owner) * 256 + position) * 256 + tile
    smem = pl.BlockSpec(memory_space=pltpu.SMEM)
    return pl.pallas_call(
        functools.partial(plan_kernel, owned),
        out_shape=(
            jax.ShapeDtypeStruct((owned, heads * slots + PLAN_UNROLL), jnp.int32),
            jax.ShapeDtypeStruct((owned, heads + 1), jnp.int32),
        ),
        in_specs=[smem, smem],
        out_specs=(smem, smem),
        compiler_params=pltpu.CompilerParams(vmem_limit_bytes=1024 * 1024),
        name="plan",
    )(codes, counts)


def attend_kernel(chunk, sources, entries, starts, *refs):
    blocks = 1 + max(i for pieces in sources for i, _ in pieces)
    q_hbm = refs[:blocks]
    k_hbm, v_hbm, out_ref, qs, ks, vs, acc, top, den, stats, sems = refs[blocks:]
    heads, _, width = qs.shape
    owners = qs.shape[1] // BLOCK
    scale = width**-0.5 * math.log2(math.e)

    def copies(h):
        moves = [(k_hbm.at[:, h * width : (h + 1) * width], ks.at[h])]
        moves.append((v_hbm.at[:, h * width : (h + 1) * width], vs.at[h]))
        for n, (i, lane) in enumerate(sources[h]):
            rows = q_hbm[i].shape[0]
            src = q_hbm[i].at[:, lane * width : (lane + 1) * width]
            moves.append((src, qs.at[h, n * rows : (n + 1) * rows]))
        return [
            pltpu.make_async_copy(src, dst, sems.at[h, i]) for i, (src, dst) in enumerate(moves)
        ]

    for h in range(heads):
        for copy in copies(h):
            copy.start()
    acc[...] = jnp.zeros_like(acc)
    den[...] = jnp.zeros_like(den)
    top[...] = jnp.full_like(top, -jnp.inf)
    count = starts[chunk, heads]
    groups = lax.div(count + UNROLL - 1, jnp.int32(UNROLL))
    opens = [lax.div(starts[chunk, h], jnp.int32(UNROLL)) for h in range(heads)]

    def group(step, carry):
        for h in range(heads):

            @pl.when(step == opens[h])
            def _():
                for copy in copies(h):
                    copy.wait()

        slots = []
        for u in range(UNROLL):
            j = step * UNROLL + u
            live = j < count
            entry = jnp.where(live, entries[chunk, j], 0)
            head = lax.bitwise_and(lax.shift_right_logical(entry, 24), 15)
            owner = lax.bitwise_and(lax.shift_right_logical(entry, 16), 255)
            position = lax.bitwise_and(lax.shift_right_logical(entry, 8), 255)
            tile = lax.bitwise_and(entry, 255)
            slot = jnp.where(live, head * owners + owner, heads * owners)
            slots.append((slot, head, position, tile))

        def rows(i):
            return pl.ds(pl.multiple_of(i * BLOCK, BLOCK), BLOCK)

        scores = [
            lax.dot_general(
                ks[head, rows(tile), :],
                qs[head, rows(position), :],
                (((1,), (1,)), ((), ())),
                preferred_element_type=F32,
            )
            for _, head, position, tile in slots
        ]
        scores = [s * scale for s in scores]
        tops = [jnp.max(s, axis=0, keepdims=True) for s in scores]
        steps = []
        for (slot, _, _, _), m in zip(slots, tops):
            row = pl.ds(slot, 1)
            old = top[row, :]
            new = jnp.maximum(old, m)
            top[row, :] = new
            steps.append((new, jnp.exp2(old - new)))
        parts = []
        for (slot, head, _, tile), s, (new, _) in zip(slots, scores, steps):
            p = jnp.exp2(s - new)
            d = jnp.sum(p, axis=0, keepdims=True)
            o = lax.dot_general(
                vs[head, rows(tile), :],
                p.astype(BF16),
                (((0,), (0,)), ((), ())),
                preferred_element_type=F32,
            )
            parts.append((d, o))
        for (slot, _, _, _), (_, keep), (d, o) in zip(slots, steps, parts):
            row = pl.ds(slot, 1)
            den[row, :] = den[row, :] * keep + d
            acc[slot] = acc[slot] * keep + o
        return carry

    lax.fori_loop(0, groups, group, 0)
    for h in range(heads):

        @pl.when(opens[h] >= groups)
        def _():
            for copy in copies(h):
                copy.wait()

    used = heads * owners
    total = den[0:used, :]
    listed = total > 0
    safe = jnp.where(listed, total, 1.0)
    level = jnp.where(listed, top[0:used, :] + jnp.log2(safe), ABSENT)
    den[0:used, :] = jnp.where(listed, 1.0 / safe, 0.0)
    for h in range(heads):
        for q in range(owners):
            at = h * owners + q
            out_ref[q, h * width : (h + 1) * width, :] = (acc[at] * den[at : at + 1, :]).astype(BF16)
        for i, piece in enumerate(split3(level[h * owners : (h + 1) * owners])):
            stats[3 * h + i] = piece
    first = out_ref.shape[1] - STAT_ROWS
    for q in range(owners):
        rows = [stats[i, q : q + 1, :] for i in range(3 * heads)]
        rows.append(jnp.zeros((STAT_ROWS - 3 * heads, BLOCK), F32))
        out_ref[q, first:, :] = jnp.concatenate(rows, axis=0).astype(BF16)


def in_hbm(x):
    return pltpu.with_memory_space_constraint(x, pltpu.HBM)


def attend(chunk, entries, starts, queries, sources, keys, values):
    heads = len(sources)
    width = keys.shape[1] // heads
    count = sum(queries[i].shape[0] for i, _ in sources[0])
    owners = count // BLOCK
    smem = pl.BlockSpec(memory_space=pltpu.SMEM)
    hbm = pl.BlockSpec(memory_space=pl.ANY)
    lines = -(-(heads * owners + 1) // 8) * 8
    return pl.pallas_call(
        functools.partial(attend_kernel, chunk, sources),
        out_shape=jax.ShapeDtypeStruct((owners, heads * width + STAT_ROWS, BLOCK), BF16),
        in_specs=[smem, smem] + [hbm] * (len(queries) + 2),
        scratch_shapes=[
            pltpu.VMEM((heads, count, width), BF16),
            pltpu.VMEM((heads, keys.shape[0], width), BF16),
            pltpu.VMEM((heads, values.shape[0], width), BF16),
            pltpu.VMEM((heads * owners + 1, width, BLOCK), F32),
            pltpu.VMEM((lines, BLOCK), F32),
            pltpu.VMEM((lines, BLOCK), F32),
            pltpu.VMEM((3 * heads, owners, BLOCK), F32),
            pltpu.SemaphoreType.DMA((heads, 2 + max(len(p) for p in sources))),
        ],
        compiler_params=pltpu.CompilerParams(vmem_limit_bytes=40 * 1024 * 1024),
        name="attend",
    )(entries, starts, *queries, in_hbm(keys), in_hbm(values))


def project_kernel(heads, core, in_ref, weight, own_ref, other_ref, mixed, held, sems):
    ranges, total, rows = in_ref.shape
    width = (total - STAT_ROWS) // heads
    first = total - STAT_ROWS
    zs, _, span = own_ref.shape

    def copy(z, s):
        column = pl.multiple_of((2 * z + jnp.bitwise_xor(core[0], s)) * span, span)
        return pltpu.make_async_copy(
            weight.at[:, pl.ds(column, span)], held.at[z, s], sems.at[z, s]
        )

    turns = [(z, s) for z in range(zs) for s in range(2)]
    for z, s in turns:
        copy(z, s).start()
    stats = in_ref[:, first:, :].astype(F32)
    for h in range(heads):
        level = stats[:, 3 * h, :] + stats[:, 3 * h + 1, :] + stats[:, 3 * h + 2, :]
        share = jnp.exp2(level - jnp.max(level, axis=0, keepdims=True))
        share = share / jnp.sum(share, axis=0, keepdims=True)
        acc = jnp.zeros((width, rows), F32)
        for r in range(ranges):
            acc += in_ref[r, h * width : (h + 1) * width, :].astype(F32) * share[r : r + 1, :]
        mixed[h * width : (h + 1) * width, :] = acc.astype(BF16)
    for z, s in turns:
        copy(z, s).wait()
        (own_ref, other_ref)[s][z] = lax.dot_general(
            mixed[...], held[z, s], (((0,), (0,)), ((), ())), preferred_element_type=F32
        ).astype(BF16)


def project(core, parts, weight, heads, span):
    depth = weight.shape[0]
    zs = weight.shape[1] // span // 2
    rows = parts.shape[2]
    result = pl.BlockSpec((zs, rows, span), lambda i, core: (0, 0, 0))
    return pl.pallas_call(
        functools.partial(project_kernel, heads),
        out_shape=[jax.ShapeDtypeStruct((zs, rows, span), BF16)] * 2,
        grid_spec=pltpu.PrefetchScalarGridSpec(
            num_scalar_prefetch=1,
            grid=(1,),
            in_specs=[
                pl.BlockSpec(parts.shape, lambda i, core: (0, 0, 0)),
                pl.BlockSpec(memory_space=pl.ANY),
            ],
            out_specs=[result, result],
            scratch_shapes=[
                pltpu.VMEM((depth, rows), BF16),
                pltpu.VMEM((zs, 2, depth, span), BF16),
                pltpu.SemaphoreType.DMA((zs, 2)),
            ],
        ),
        compiler_params=pltpu.CompilerParams(vmem_limit_bytes=24 * 1024 * 1024),
        name="project",
    )(core, parts, in_hbm(weight))


def pair_kernel(z, mine, theirs, own, *others):
    zs = mine.shape[0]
    for d, out in zip((0,) + Z_STEPS, (own,) + others):
        at = lax.rem(z[0] + d, jnp.int32(zs))
        out[...] = (mine[at].astype(F32) + theirs[at].astype(F32)).astype(out.dtype)


def pair(z, mine, theirs):
    shape = mine.shape[1:]
    whole = pl.BlockSpec(mine.shape, lambda i, z: (0, 0, 0))
    return pl.pallas_call(
        pair_kernel,
        out_shape=[jax.ShapeDtypeStruct(shape, F32)]
        + [jax.ShapeDtypeStruct(shape, BF16) for _ in Z_STEPS],
        grid_spec=pltpu.PrefetchScalarGridSpec(
            num_scalar_prefetch=1,
            grid=(1,),
            in_specs=[whole, whole],
            out_specs=[pl.BlockSpec(shape, lambda i, z: (0, 0))] * (1 + len(Z_STEPS)),
        ),
        compiler_params=pltpu.CompilerParams(vmem_limit_bytes=8 * 1024 * 1024),
        name="pair",
    )(z, mine, theirs)


def local(queries, key_states, value_states, block_ids, block_counts, out_weight):
    heads = block_ids.shape[0]
    ranges = lax.axis_size("keys")
    groups = lax.axis_size("heads")
    me = lax.axis_index("heads")
    core = jnp.reshape(me % 2, (1,)).astype(jnp.int32)
    z = jnp.reshape(me // 2, (1,)).astype(jnp.int32)
    span = out_weight.shape[1] // groups
    tiles = key_states.shape[0] // BLOCK
    owned = queries.shape[0] // BLOCK
    side = math.isqrt(ranges)

    def exchange(parts):
        return lax.all_to_all(parts, "keys", split_axis=0, concat_axis=0, tiled=True)

    def finish(got):
        mine, theirs = project(core, got, out_weight, heads, span)
        swap = [(g, g ^ 1) for g in range(groups)]
        own, *others = pair(z, mine, lax.ppermute(theirs, "heads", swap))
        total = own
        for d, piece in zip(Z_STEPS, others):
            pairs = [(g, (g + 2 * d) % groups) for g in range(groups)]
            total = total + lax.ppermute(piece, "heads", pairs).astype(F32)
        return total.astype(BF16)

    def rows(c):
        return queries[c * BLOCK : (c + 1) * BLOCK]

    def along(x, axis):
        def pairs(d):
            there = lambda i, j: ((i + d) % side, j) if axis == 0 else (i, (j + d) % side)
            moved = [there(k // side, k % side) for k in range(ranges)]
            return [(k, i * side + j) for k, (i, j) in enumerate(moved)]

        got = {d: lax.ppermute(x, "keys", pairs(d)) for d in Z_STEPS}
        return [x] + [got[d] for d in range(1, side)]

    near = rows(0)
    middle = near.shape[1] // 2
    left, right = near[:, :middle], near[:, middle:]
    left, right = lax.optimization_barrier((left, right))
    halves = along(left, 0) + along(right, 1)
    halves = lax.optimization_barrier(halves)
    left, right = jnp.concatenate(halves[:side]), jnp.concatenate(halves[side:])
    left, right = lax.optimization_barrier((left, right))
    direct = lax.optimization_barrier(along(left, 1) + along(right, 0))
    lower = [[(i, h) for i in range(side)] for h in range(heads // 2)]
    upper = [[(side + i, h) for i in range(side)] for h in range(heads // 2)]
    whole = [[(0, h)] for h in range(heads)]

    slot = jnp.reshape(lax.axis_index("keys"), (1,)).astype(jnp.int32)
    entries, starts = plan(slot, block_ids, block_counts, tiles, owned, side)
    outs = []
    for c in range(owned):
        if c == 0:
            source, lanes = direct, lower + upper
        else:
            source, lanes = [in_hbm(lax.all_gather(rows(c), "keys", axis=0, tiled=True))], whole
        parts = attend(c, entries, starts, source, lanes, key_states, value_states)
        got = exchange(parts)
        if outs:
            got, outs[-1] = lax.optimization_barrier((got, outs[-1]))
        outs.append(finish(got))
    return jnp.concatenate(outs)


def solution(mesh):
    in_specs = (
        P("keys", "heads"),
        P("keys", "heads"),
        P("keys", "heads"),
        P("heads", "keys"),
        P("heads", "keys"),
        P("heads", None),
    )
    return jax.shard_map(
        local, mesh=mesh, in_specs=in_specs, out_specs=P("keys", "heads"), check_vma=False
    )
```

```python
import functools
import math

import jax
import jax.numpy as jnp
from jax import lax
from jax.experimental import pallas as pl
from jax.experimental.pallas import tpu as pltpu
from jax.sharding import PartitionSpec as P

BLOCK = 128
UNROLL = 16
PLAN_UNROLL = 8
CHUNK_BIT = 28
STAT_ROWS = 16
ABSENT = -3.0e38
Z_STEPS = (1, 3, 2)
F32 = jnp.float32
BF16 = jnp.bfloat16


def split3(x):
    high = x.astype(BF16).astype(F32)
    rest = x - high
    middle = rest.astype(BF16).astype(F32)
    return high, middle, rest - middle


def plan_kernel(owned, codes, counts, entries, starts):
    heads = codes.shape[0]

    def over_head(h, at):
        for c in range(owned):
            starts[c, h] = at[c]
        count = counts[h, 0]

        def some(step, at):
            for u in range(PLAN_UNROLL):
                j = step * PLAN_UNROLL + u
                code = codes[h, j]
                chunk = lax.shift_right_logical(code, CHUNK_BIT)
                place = at[0]
                for c in range(1, owned):
                    place = jnp.where(chunk == c, at[c], place)
                entries[chunk, place] = code
                live = j < count
                at = tuple(
                    a + jnp.where(live & (chunk == c), 1, 0) for c, a in enumerate(at)
                )
            return at

        return lax.fori_loop(0, lax.div(count + PLAN_UNROLL - 1, PLAN_UNROLL), some, at)

    at = lax.fori_loop(0, heads, over_head, (jnp.int32(0),) * owned)
    for c in range(owned):
        starts[c, heads] = at[c]


def plan(me, ids, counts, tiles, owned, side):
    heads, slots = ids.shape
    query, tile = ids // tiles, ids % tiles
    owner, chunk = query // owned, query % owned
    dx = (me // side - owner // side) % side
    dy = (me % side - owner % side) % side
    head = jnp.arange(heads, dtype=jnp.int32)[:, None]
    position = jnp.where(head < heads // 2, dy * side + dx, dx * side + dy)
    codes = (((chunk * 16 + head) * 256 + owner) * 256 + position) * 256 + tile
    smem = pl.BlockSpec(memory_space=pltpu.SMEM)
    return pl.pallas_call(
        functools.partial(plan_kernel, owned),
        out_shape=(
            jax.ShapeDtypeStruct((owned, heads * slots + PLAN_UNROLL), jnp.int32),
            jax.ShapeDtypeStruct((owned, heads + 1), jnp.int32),
        ),
        in_specs=[smem, smem],
        out_specs=(smem, smem),
        compiler_params=pltpu.CompilerParams(vmem_limit_bytes=1024 * 1024),
        name="plan",
    )(codes, counts)


def regroup_kernel(side, *refs):
    pieces, lines = refs[: 2 * side], refs[2 * side :]
    for n, line in enumerate(lines):
        chunk, half = divmod(n, 2)
        for d in range(side):
            piece = pieces[half * side + d]
            line[d * BLOCK : (d + 1) * BLOCK] = piece[chunk * BLOCK : (chunk + 1) * BLOCK]


def regroup(halves, side, owned):
    vmem = pl.BlockSpec(memory_space=pltpu.VMEM)
    line = jax.ShapeDtypeStruct((side * BLOCK, halves[0].shape[1]), BF16)
    lines = pl.pallas_call(
        functools.partial(regroup_kernel, side),
        out_shape=[line] * (2 * owned),
        in_specs=[vmem] * (2 * side),
        out_specs=[vmem] * (2 * owned),
        compiler_params=pltpu.CompilerParams(vmem_limit_bytes=8 * 1024 * 1024),
        name="regroup",
    )(*halves)
    return [(lines[2 * c], lines[2 * c + 1]) for c in range(owned)]


def attend_kernel(chunk, sources, entries, starts, *refs):
    blocks = 1 + max(i for pieces in sources for i, _ in pieces)
    q_hbm = refs[:blocks]
    k_hbm, v_hbm, out_ref, qs, ks, vs, acc, top, den, stats, sems = refs[blocks:]
    heads, _, width = qs.shape
    owners = qs.shape[1] // BLOCK
    scale = width**-0.5 * math.log2(math.e)

    def copies(h):
        moves = [(k_hbm.at[:, h * width : (h + 1) * width], ks.at[h])]
        moves.append((v_hbm.at[:, h * width : (h + 1) * width], vs.at[h]))
        for n, (i, lane) in enumerate(sources[h]):
            rows = q_hbm[i].shape[0]
            src = q_hbm[i].at[:, lane * width : (lane + 1) * width]
            moves.append((src, qs.at[h, n * rows : (n + 1) * rows]))
        return [
            pltpu.make_async_copy(src, dst, sems.at[h, i]) for i, (src, dst) in enumerate(moves)
        ]

    for h in range(heads):
        for copy in copies(h):
            copy.start()
    acc[...] = jnp.zeros_like(acc)
    den[...] = jnp.zeros_like(den)
    top[...] = jnp.full_like(top, -jnp.inf)
    count = starts[chunk, heads]
    groups = lax.div(count + UNROLL - 1, jnp.int32(UNROLL))
    opens = [lax.div(starts[chunk, h], jnp.int32(UNROLL)) for h in range(heads)]

    def group(step, carry):
        for h in range(heads):

            @pl.when(step == opens[h])
            def _():
                for copy in copies(h):
                    copy.wait()

        slots = []
        for u in range(UNROLL):
            j = step * UNROLL + u
            live = j < count
            entry = jnp.where(live, entries[chunk, j], 0)
            head = lax.bitwise_and(lax.shift_right_logical(entry, 24), 15)
            owner = lax.bitwise_and(lax.shift_right_logical(entry, 16), 255)
            position = lax.bitwise_and(lax.shift_right_logical(entry, 8), 255)
            tile = lax.bitwise_and(entry, 255)
            slot = jnp.where(live, head * owners + owner, heads * owners)
            slots.append((slot, head, position, tile))

        def rows(i):
            return pl.ds(pl.multiple_of(i * BLOCK, BLOCK), BLOCK)

        scores = [
            lax.dot_general(
                ks[head, rows(tile), :],
                qs[head, rows(position), :],
                (((1,), (1,)), ((), ())),
                preferred_element_type=F32,
            )
            for _, head, position, tile in slots
        ]
        scores = [s * scale for s in scores]
        tops = [jnp.max(s, axis=0, keepdims=True) for s in scores]
        steps = []
        for (slot, _, _, _), m in zip(slots, tops):
            row = pl.ds(slot, 1)
            old = top[row, :]
            new = jnp.maximum(old, m)
            top[row, :] = new
            steps.append((new, jnp.exp2(old - new)))
        parts = []
        for (slot, head, _, tile), s, (new, _) in zip(slots, scores, steps):
            p = jnp.exp2(s - new)
            d = jnp.sum(p, axis=0, keepdims=True)
            o = lax.dot_general(
                vs[head, rows(tile), :],
                p.astype(BF16),
                (((0,), (0,)), ((), ())),
                preferred_element_type=F32,
            )
            parts.append((d, o))
        for (slot, _, _, _), (_, keep), (d, o) in zip(slots, steps, parts):
            row = pl.ds(slot, 1)
            den[row, :] = den[row, :] * keep + d
            acc[slot] = acc[slot] * keep + o
        return carry

    lax.fori_loop(0, groups, group, 0)
    for h in range(heads):

        @pl.when(opens[h] >= groups)
        def _():
            for copy in copies(h):
                copy.wait()

    used = heads * owners
    total = den[0:used, :]
    listed = total > 0
    safe = jnp.where(listed, total, 1.0)
    level = jnp.where(listed, top[0:used, :] + jnp.log2(safe), ABSENT)
    den[0:used, :] = jnp.where(listed, 1.0 / safe, 0.0)
    for h in range(heads):
        for q in range(owners):
            at = h * owners + q
            out_ref[q, h * width : (h + 1) * width, :] = (acc[at] * den[at : at + 1, :]).astype(BF16)
        for i, piece in enumerate(split3(level[h * owners : (h + 1) * owners])):
            stats[3 * h + i] = piece
    first = out_ref.shape[1] - STAT_ROWS
    for q in range(owners):
        rows = [stats[i, q : q + 1, :] for i in range(3 * heads)]
        rows.append(jnp.zeros((STAT_ROWS - 3 * heads, BLOCK), F32))
        out_ref[q, first:, :] = jnp.concatenate(rows, axis=0).astype(BF16)


def in_hbm(x):
    return pltpu.with_memory_space_constraint(x, pltpu.HBM)


def attend(chunk, entries, starts, queries, sources, keys, values):
    heads = len(sources)
    width = keys.shape[1] // heads
    count = sum(queries[i].shape[0] for i, _ in sources[0])
    owners = count // BLOCK
    smem = pl.BlockSpec(memory_space=pltpu.SMEM)
    hbm = pl.BlockSpec(memory_space=pl.ANY)
    lines = -(-(heads * owners + 1) // 8) * 8
    return pl.pallas_call(
        functools.partial(attend_kernel, chunk, sources),
        out_shape=jax.ShapeDtypeStruct((owners, heads * width + STAT_ROWS, BLOCK), BF16),
        in_specs=[smem, smem] + [hbm] * (len(queries) + 2),
        scratch_shapes=[
            pltpu.VMEM((heads, count, width), BF16),
            pltpu.VMEM((heads, keys.shape[0], width), BF16),
            pltpu.VMEM((heads, values.shape[0], width), BF16),
            pltpu.VMEM((heads * owners + 1, width, BLOCK), F32),
            pltpu.VMEM((lines, BLOCK), F32),
            pltpu.VMEM((lines, BLOCK), F32),
            pltpu.VMEM((3 * heads, owners, BLOCK), F32),
            pltpu.SemaphoreType.DMA((heads, 2 + max(len(p) for p in sources))),
        ],
        compiler_params=pltpu.CompilerParams(vmem_limit_bytes=28 * 1024 * 1024),
        name="attend",
    )(entries, starts, *queries, in_hbm(keys), in_hbm(values))


def project_kernel(heads, core, in_ref, weight, own_ref, other_ref, mixed, held, sems):
    ranges, total, rows = in_ref.shape
    width = (total - STAT_ROWS) // heads
    first = total - STAT_ROWS
    zs, _, span = own_ref.shape

    def copy(z, s):
        column = pl.multiple_of((2 * z + jnp.bitwise_xor(core[0], s)) * span, span)
        return pltpu.make_async_copy(
            weight.at[:, pl.ds(column, span)], held.at[z, s], sems.at[z, s]
        )

    turns = [(z, s) for z in range(zs) for s in range(2)]
    for z, s in turns:
        copy(z, s).start()
    stats = in_ref[:, first:, :].astype(F32)
    for h in range(heads):
        level = stats[:, 3 * h, :] + stats[:, 3 * h + 1, :] + stats[:, 3 * h + 2, :]
        share = jnp.exp2(level - jnp.max(level, axis=0, keepdims=True))
        share = share / jnp.sum(share, axis=0, keepdims=True)
        acc = jnp.zeros((width, rows), F32)
        for r in range(ranges):
            acc += in_ref[r, h * width : (h + 1) * width, :].astype(F32) * share[r : r + 1, :]
        mixed[h * width : (h + 1) * width, :] = acc.astype(BF16)
    for z, s in turns:
        copy(z, s).wait()
        (own_ref, other_ref)[s][z] = lax.dot_general(
            mixed[...], held[z, s], (((0,), (0,)), ((), ())), preferred_element_type=F32
        ).astype(BF16)


def project(core, parts, weight, heads, span):
    depth = weight.shape[0]
    zs = weight.shape[1] // span // 2
    rows = parts.shape[2]
    result = pl.BlockSpec((zs, rows, span), lambda i, core: (0, 0, 0))
    return pl.pallas_call(
        functools.partial(project_kernel, heads),
        out_shape=[jax.ShapeDtypeStruct((zs, rows, span), BF16)] * 2,
        grid_spec=pltpu.PrefetchScalarGridSpec(
            num_scalar_prefetch=1,
            grid=(1,),
            in_specs=[
                pl.BlockSpec(parts.shape, lambda i, core: (0, 0, 0)),
                pl.BlockSpec(memory_space=pl.ANY),
            ],
            out_specs=[result, result],
            scratch_shapes=[
                pltpu.VMEM((depth, rows), BF16),
                pltpu.VMEM((zs, 2, depth, span), BF16),
                pltpu.SemaphoreType.DMA((zs, 2)),
            ],
        ),
        compiler_params=pltpu.CompilerParams(vmem_limit_bytes=14 * 1024 * 1024),
        name="project",
    )(core, parts, in_hbm(weight))


def pair_kernel(z, mine, theirs, own, *others):
    zs = mine.shape[0]
    for d, out in zip((0,) + Z_STEPS, (own,) + others):
        at = lax.rem(z[0] + d, jnp.int32(zs))
        out[...] = (mine[at].astype(F32) + theirs[at].astype(F32)).astype(out.dtype)


def pair(z, mine, theirs):
    shape = mine.shape[1:]
    whole = pl.BlockSpec(mine.shape, lambda i, z: (0, 0, 0))
    return pl.pallas_call(
        pair_kernel,
        out_shape=[jax.ShapeDtypeStruct(shape, F32)]
        + [jax.ShapeDtypeStruct(shape, BF16) for _ in Z_STEPS],
        grid_spec=pltpu.PrefetchScalarGridSpec(
            num_scalar_prefetch=1,
            grid=(1,),
            in_specs=[whole, whole],
            out_specs=[pl.BlockSpec(shape, lambda i, z: (0, 0))] * (1 + len(Z_STEPS)),
        ),
        compiler_params=pltpu.CompilerParams(vmem_limit_bytes=8 * 1024 * 1024),
        name="pair",
    )(z, mine, theirs)


def local(queries, key_states, value_states, block_ids, block_counts, out_weight):
    heads = block_ids.shape[0]
    ranges = lax.axis_size("keys")
    groups = lax.axis_size("heads")
    me = lax.axis_index("heads")
    core = jnp.reshape(me % 2, (1,)).astype(jnp.int32)
    z = jnp.reshape(me // 2, (1,)).astype(jnp.int32)
    span = out_weight.shape[1] // groups
    tiles = key_states.shape[0] // BLOCK
    owned = queries.shape[0] // BLOCK
    side = math.isqrt(ranges)

    def exchange(parts):
        return lax.all_to_all(parts, "keys", split_axis=0, concat_axis=0, tiled=True)

    def finish(got):
        mine, theirs = project(core, got, out_weight, heads, span)
        swap = [(g, g ^ 1) for g in range(groups)]
        own, *others = pair(z, mine, lax.ppermute(theirs, "heads", swap))
        total = own
        for d, piece in zip(Z_STEPS, others):
            pairs = [(g, (g + 2 * d) % groups) for g in range(groups)]
            total = total + lax.ppermute(piece, "heads", pairs).astype(F32)
        return total.astype(BF16)

    def along(x, axis):
        def pairs(d):
            there = lambda i, j: ((i + d) % side, j) if axis == 0 else (i, (j + d) % side)
            moved = [there(k // side, k % side) for k in range(ranges)]
            return [(k, i * side + j) for k, (i, j) in enumerate(moved)]

        got = {d: lax.ppermute(x, "keys", pairs(d)) for d in Z_STEPS}
        return [x] + [got[d] for d in range(1, side)]

    middle = queries.shape[1] // 2
    left, right = queries[:, :middle], queries[:, middle:]
    left, right = lax.optimization_barrier((left, right))
    halves = lax.optimization_barrier(along(left, 0) + along(right, 1))

    sources = []
    for left, right in regroup(halves, side, owned):
        sources.append(lax.optimization_barrier(along(left, 1) + along(right, 0)))
    lower = [[(i, h) for i in range(side)] for h in range(heads // 2)]
    upper = [[(side + i, h) for i in range(side)] for h in range(heads // 2)]

    slot = jnp.reshape(lax.axis_index("keys"), (1,)).astype(jnp.int32)
    entries, starts = plan(slot, block_ids, block_counts, tiles, owned, side)
    outs = []
    for c in range(owned):
        parts = attend(
            c, entries, starts, sources[c], lower + upper, key_states, value_states
        )
        got = exchange(parts)
        if outs:
            got, outs[-1] = lax.optimization_barrier((got, outs[-1]))
        outs.append(finish(got))
    return jnp.concatenate(outs)


def solution(mesh):
    in_specs = (
        P("keys", "heads"),
        P("keys", "heads"),
        P("keys", "heads"),
        P("heads", "keys"),
        P("heads", "keys"),
        P("heads", None),
    )
    return jax.shard_map(
        local, mesh=mesh, in_specs=in_specs, out_specs=P("keys", "heads"), check_vma=False
    )
```

```python
import functools
import math

import jax
import jax.numpy as jnp
from jax import lax
from jax.experimental import pallas as pl
from jax.experimental.pallas import tpu as pltpu
from jax.sharding import PartitionSpec as P

BLOCK = 128
UNROLL = 16
PLAN_UNROLL = 8
CHUNK_BIT = 28
STAT_ROWS = 16
ABSENT = -3.0e38
Z_STEPS = (1, 3, 2)
F32 = jnp.float32
BF16 = jnp.bfloat16


def split3(x):
    high = x.astype(BF16).astype(F32)
    rest = x - high
    middle = rest.astype(BF16).astype(F32)
    return high, middle, rest - middle


def plan_kernel(owned, codes, counts, entries, starts):
    heads = codes.shape[0]

    def over_head(h, at):
        for c in range(owned):
            starts[c, h] = at[c]
        count = counts[h, 0]

        def some(step, at):
            for u in range(PLAN_UNROLL):
                j = step * PLAN_UNROLL + u
                code = codes[h, j]
                chunk = lax.shift_right_logical(code, CHUNK_BIT)
                place = at[0]
                for c in range(1, owned):
                    place = jnp.where(chunk == c, at[c], place)
                entries[chunk, place] = code
                live = j < count
                at = tuple(
                    a + jnp.where(live & (chunk == c), 1, 0) for c, a in enumerate(at)
                )
            return at

        return lax.fori_loop(0, lax.div(count + PLAN_UNROLL - 1, PLAN_UNROLL), some, at)

    at = lax.fori_loop(0, heads, over_head, (jnp.int32(0),) * owned)
    for c in range(owned):
        starts[c, heads] = at[c]


def plan(me, ids, counts, tiles, owned, side):
    heads, slots = ids.shape
    query, tile = ids // tiles, ids % tiles
    owner, chunk = query // owned, query % owned
    dx = (me // side - owner // side) % side
    dy = (me % side - owner % side) % side
    head = jnp.arange(heads, dtype=jnp.int32)[:, None]
    position = jnp.where(head < heads // 2, dy * side + dx, dx * side + dy)
    codes = (((chunk * 16 + head) * 256 + owner) * 256 + position) * 256 + tile
    smem = pl.BlockSpec(memory_space=pltpu.SMEM)
    return pl.pallas_call(
        functools.partial(plan_kernel, owned),
        out_shape=(
            jax.ShapeDtypeStruct((owned, heads * slots + PLAN_UNROLL), jnp.int32),
            jax.ShapeDtypeStruct((owned, heads + 1), jnp.int32),
        ),
        in_specs=[smem, smem],
        out_specs=(smem, smem),
        compiler_params=pltpu.CompilerParams(vmem_limit_bytes=1024 * 1024),
        name="plan",
    )(codes, counts)


def attend_kernel(chunk, sources, entries, starts, *refs):
    blocks = 1 + max(i for pieces in sources for i, _ in pieces)
    q_hbm = refs[:blocks]
    k_hbm, v_hbm, out_ref, qs, ks, vs, acc, top, den, stats, sems = refs[blocks:]
    heads, owners, _, width = qs.shape
    scale = width**-0.5 * math.log2(math.e)

    def copies(h):
        moves = [(k_hbm.at[:, h * width : (h + 1) * width], ks.at[h])]
        moves.append((v_hbm.at[:, h * width : (h + 1) * width], vs.at[h]))
        for n, (i, lane) in enumerate(sources[h]):
            blocks = q_hbm[i].shape[0]
            src = q_hbm[i].at[:, chunk, :, lane * width : (lane + 1) * width]
            moves.append((src, qs.at[h, n * blocks : (n + 1) * blocks]))
        return [
            pltpu.make_async_copy(src, dst, sems.at[h, i]) for i, (src, dst) in enumerate(moves)
        ]

    for h in range(heads):
        for copy in copies(h):
            copy.start()
    acc[...] = jnp.zeros_like(acc)
    den[...] = jnp.zeros_like(den)
    top[...] = jnp.full_like(top, -jnp.inf)
    count = starts[chunk, heads]
    groups = lax.div(count + UNROLL - 1, jnp.int32(UNROLL))
    opens = [lax.div(starts[chunk, h], jnp.int32(UNROLL)) for h in range(heads)]

    def group(step, carry):
        for h in range(heads):

            @pl.when(step == opens[h])
            def _():
                for copy in copies(h):
                    copy.wait()

        slots = []
        for u in range(UNROLL):
            j = step * UNROLL + u
            live = j < count
            entry = jnp.where(live, entries[chunk, j], 0)
            head = lax.bitwise_and(lax.shift_right_logical(entry, 24), 15)
            owner = lax.bitwise_and(lax.shift_right_logical(entry, 16), 255)
            position = lax.bitwise_and(lax.shift_right_logical(entry, 8), 255)
            tile = lax.bitwise_and(entry, 255)
            slot = jnp.where(live, head * owners + owner, heads * owners)
            slots.append((slot, head, position, tile))

        def rows(i):
            return pl.ds(pl.multiple_of(i * BLOCK, BLOCK), BLOCK)

        scores = [
            lax.dot_general(
                ks[head, rows(tile), :],
                qs[head, position],
                (((1,), (1,)), ((), ())),
                preferred_element_type=F32,
            )
            for _, head, position, tile in slots
        ]
        scores = [s * scale for s in scores]
        tops = [jnp.max(s, axis=0, keepdims=True) for s in scores]
        steps = []
        for (slot, _, _, _), m in zip(slots, tops):
            row = pl.ds(slot, 1)
            old = top[row, :]
            new = jnp.maximum(old, m)
            top[row, :] = new
            steps.append((new, jnp.exp2(old - new)))
        parts = []
        for (slot, head, _, tile), s, (new, _) in zip(slots, scores, steps):
            p = jnp.exp2(s - new)
            d = jnp.sum(p, axis=0, keepdims=True)
            o = lax.dot_general(
                vs[head, rows(tile), :],
                p.astype(BF16),
                (((0,), (0,)), ((), ())),
                preferred_element_type=F32,
            )
            parts.append((d, o))
        for (slot, _, _, _), (_, keep), (d, o) in zip(slots, steps, parts):
            row = pl.ds(slot, 1)
            den[row, :] = den[row, :] * keep + d
            acc[slot] = acc[slot] * keep + o
        return carry

    lax.fori_loop(0, groups, group, 0)
    for h in range(heads):

        @pl.when(opens[h] >= groups)
        def _():
            for copy in copies(h):
                copy.wait()

    used = heads * owners
    total = den[0:used, :]
    listed = total > 0
    safe = jnp.where(listed, total, 1.0)
    level = jnp.where(listed, top[0:used, :] + jnp.log2(safe), ABSENT)
    den[0:used, :] = jnp.where(listed, 1.0 / safe, 0.0)
    for h in range(heads):
        for q in range(owners):
            at = h * owners + q
            out_ref[q, h * width : (h + 1) * width, :] = (acc[at] * den[at : at + 1, :]).astype(BF16)
        for i, piece in enumerate(split3(level[h * owners : (h + 1) * owners])):
            stats[3 * h + i] = piece
    first = out_ref.shape[1] - STAT_ROWS
    for q in range(owners):
        rows = [stats[i, q : q + 1, :] for i in range(3 * heads)]
        rows.append(jnp.zeros((STAT_ROWS - 3 * heads, BLOCK), F32))
        out_ref[q, first:, :] = jnp.concatenate(rows, axis=0).astype(BF16)


def in_hbm(x):
    return pltpu.with_memory_space_constraint(x, pltpu.HBM)


def attend(chunk, entries, starts, queries, sources, keys, values):
    heads = len(sources)
    width = keys.shape[1] // heads
    owners = sum(queries[i].shape[0] for i, _ in sources[0])
    smem = pl.BlockSpec(memory_space=pltpu.SMEM)
    hbm = pl.BlockSpec(memory_space=pl.ANY)
    lines = -(-(heads * owners + 1) // 8) * 8
    return pl.pallas_call(
        functools.partial(attend_kernel, chunk, sources),
        out_shape=jax.ShapeDtypeStruct((owners, heads * width + STAT_ROWS, BLOCK), BF16),
        in_specs=[smem, smem] + [hbm] * (len(queries) + 2),
        scratch_shapes=[
            pltpu.VMEM((heads, owners, BLOCK, width), BF16),
            pltpu.VMEM((heads, keys.shape[0], width), BF16),
            pltpu.VMEM((heads, values.shape[0], width), BF16),
            pltpu.VMEM((heads * owners + 1, width, BLOCK), F32),
            pltpu.VMEM((lines, BLOCK), F32),
            pltpu.VMEM((lines, BLOCK), F32),
            pltpu.VMEM((3 * heads, owners, BLOCK), F32),
            pltpu.SemaphoreType.DMA((heads, 2 + max(len(p) for p in sources))),
        ],
        compiler_params=pltpu.CompilerParams(vmem_limit_bytes=50 * 1024 * 1024),
        name="attend",
    )(entries, starts, *queries, in_hbm(keys), in_hbm(values))


def project_kernel(heads, core, in_ref, weight, own_ref, other_ref, mixed, held, sems):
    ranges, total, rows = in_ref.shape
    width = (total - STAT_ROWS) // heads
    first = total - STAT_ROWS
    zs, _, span = own_ref.shape

    def copy(z, s):
        column = pl.multiple_of((2 * z + jnp.bitwise_xor(core[0], s)) * span, span)
        return pltpu.make_async_copy(
            weight.at[:, pl.ds(column, span)], held.at[z, s], sems.at[z, s]
        )

    turns = [(z, s) for z in range(zs) for s in range(2)]
    for z, s in turns:
        copy(z, s).start()
    stats = in_ref[:, first:, :].astype(F32)
    for h in range(heads):
        level = stats[:, 3 * h, :] + stats[:, 3 * h + 1, :] + stats[:, 3 * h + 2, :]
        share = jnp.exp2(level - jnp.max(level, axis=0, keepdims=True))
        share = share / jnp.sum(share, axis=0, keepdims=True)
        acc = jnp.zeros((width, rows), F32)
        for r in range(ranges):
            acc += in_ref[r, h * width : (h + 1) * width, :].astype(F32) * share[r : r + 1, :]
        mixed[h * width : (h + 1) * width, :] = acc.astype(BF16)
    for z, s in turns:
        copy(z, s).wait()
        (own_ref, other_ref)[s][z] = lax.dot_general(
            mixed[...], held[z, s], (((0,), (0,)), ((), ())), preferred_element_type=F32
        ).astype(BF16)


def project(core, parts, weight, heads, span):
    depth = weight.shape[0]
    zs = weight.shape[1] // span // 2
    rows = parts.shape[2]
    result = pl.BlockSpec((zs, rows, span), lambda i, core: (0, 0, 0))
    return pl.pallas_call(
        functools.partial(project_kernel, heads),
        out_shape=[jax.ShapeDtypeStruct((zs, rows, span), BF16)] * 2,
        grid_spec=pltpu.PrefetchScalarGridSpec(
            num_scalar_prefetch=1,
            grid=(1,),
            in_specs=[
                pl.BlockSpec(parts.shape, lambda i, core: (0, 0, 0)),
                pl.BlockSpec(memory_space=pl.ANY),
            ],
            out_specs=[result, result],
            scratch_shapes=[
                pltpu.VMEM((depth, rows), BF16),
                pltpu.VMEM((zs, 2, depth, span), BF16),
                pltpu.SemaphoreType.DMA((zs, 2)),
            ],
        ),
        compiler_params=pltpu.CompilerParams(vmem_limit_bytes=14 * 1024 * 1024),
        name="project",
    )(core, parts, in_hbm(weight))


def pair_kernel(z, mine, theirs, own, *others):
    zs = mine.shape[0]
    for d, out in zip((0,) + Z_STEPS, (own,) + others):
        at = lax.rem(z[0] + d, jnp.int32(zs))
        out[...] = (mine[at].astype(F32) + theirs[at].astype(F32)).astype(out.dtype)


def pair(z, mine, theirs):
    shape = mine.shape[1:]
    whole = pl.BlockSpec(mine.shape, lambda i, z: (0, 0, 0))
    return pl.pallas_call(
        pair_kernel,
        out_shape=[jax.ShapeDtypeStruct(shape, F32)]
        + [jax.ShapeDtypeStruct(shape, BF16) for _ in Z_STEPS],
        grid_spec=pltpu.PrefetchScalarGridSpec(
            num_scalar_prefetch=1,
            grid=(1,),
            in_specs=[whole, whole],
            out_specs=[pl.BlockSpec(shape, lambda i, z: (0, 0))] * (1 + len(Z_STEPS)),
        ),
        compiler_params=pltpu.CompilerParams(vmem_limit_bytes=8 * 1024 * 1024),
        name="pair",
    )(z, mine, theirs)


def local(queries, key_states, value_states, block_ids, block_counts, out_weight):
    heads = block_ids.shape[0]
    ranges = lax.axis_size("keys")
    groups = lax.axis_size("heads")
    me = lax.axis_index("heads")
    core = jnp.reshape(me % 2, (1,)).astype(jnp.int32)
    z = jnp.reshape(me // 2, (1,)).astype(jnp.int32)
    span = out_weight.shape[1] // groups
    tiles = key_states.shape[0] // BLOCK
    owned = queries.shape[0] // BLOCK
    side = math.isqrt(ranges)

    def exchange(parts):
        return lax.all_to_all(parts, "keys", split_axis=0, concat_axis=0, tiled=True)

    def finish(got):
        mine, theirs = project(core, got, out_weight, heads, span)
        swap = [(g, g ^ 1) for g in range(groups)]
        own, *others = pair(z, mine, lax.ppermute(theirs, "heads", swap))
        total = own
        for d, piece in zip(Z_STEPS, others):
            pairs = [(g, (g + 2 * d) % groups) for g in range(groups)]
            total = total + lax.ppermute(piece, "heads", pairs).astype(F32)
        return total.astype(BF16)

    def along(x, axis):
        def pairs(d):
            there = lambda i, j: ((i + d) % side, j) if axis == 0 else (i, (j + d) % side)
            moved = [there(k // side, k % side) for k in range(ranges)]
            return [(k, i * side + j) for k, (i, j) in enumerate(moved)]

        got = {d: lax.ppermute(x, "keys", pairs(d)) for d in Z_STEPS}
        return [x] + [got[d] for d in range(1, side)]

    middle = queries.shape[1] // 2
    left, right = queries[:, :middle], queries[:, middle:]
    left, right = lax.optimization_barrier((left, right))
    halves = lax.optimization_barrier(along(left, 0) + along(right, 1))

    left, right = jnp.concatenate(halves[:side]), jnp.concatenate(halves[side:])
    left, right = lax.optimization_barrier((left, right))
    everything = lax.optimization_barrier(along(left, 1) + along(right, 0))
    everything = [x.reshape(side, owned, BLOCK, middle) for x in everything]
    lower = [[(i, h) for i in range(side)] for h in range(heads // 2)]
    upper = [[(side + i, h) for i in range(side)] for h in range(heads // 2)]

    slot = jnp.reshape(lax.axis_index("keys"), (1,)).astype(jnp.int32)
    entries, starts = plan(slot, block_ids, block_counts, tiles, owned, side)
    outs = []
    for c in range(owned):
        parts = attend(
            c, entries, starts, everything, lower + upper, key_states, value_states
        )
        got = exchange(parts)
        if outs:
            got, outs[-1] = lax.optimization_barrier((got, outs[-1]))
        outs.append(finish(got))
    return jnp.concatenate(outs)


def solution(mesh):
    in_specs = (
        P("keys", "heads"),
        P("keys", "heads"),
        P("keys", "heads"),
        P("heads", "keys"),
        P("heads", "keys"),
        P("heads", None),
    )
    return jax.shard_map(
        local, mesh=mesh, in_specs=in_specs, out_specs=P("keys", "heads"), check_vma=False
    )
```

```python
import functools
import math

import jax
import jax.numpy as jnp
from jax import lax
from jax.experimental import pallas as pl
from jax.experimental.pallas import tpu as pltpu
from jax.sharding import PartitionSpec as P

BLOCK = 128
UNROLL = 16
PLAN_UNROLL = 8
CHUNK_BIT = 28
STAT_ROWS = 16
ABSENT = -3.0e38
Z_STEPS = (1, 3, 2)
F32 = jnp.float32
BF16 = jnp.bfloat16


def split3(x):
    high = x.astype(BF16).astype(F32)
    rest = x - high
    middle = rest.astype(BF16).astype(F32)
    return high, middle, rest - middle


def plan_kernel(owned, codes, counts, entries, starts):
    heads = codes.shape[0]

    def over_head(h, at):
        for c in range(owned):
            starts[c, h] = at[c]
        count = counts[h, 0]

        def some(step, at):
            for u in range(PLAN_UNROLL):
                j = step * PLAN_UNROLL + u
                code = codes[h, j]
                chunk = lax.shift_right_logical(code, CHUNK_BIT)
                place = at[0]
                for c in range(1, owned):
                    place = jnp.where(chunk == c, at[c], place)
                entries[chunk, place] = code
                live = j < count
                at = tuple(
                    a + jnp.where(live & (chunk == c), 1, 0) for c, a in enumerate(at)
                )
            return at

        return lax.fori_loop(0, lax.div(count + PLAN_UNROLL - 1, PLAN_UNROLL), some, at)

    at = lax.fori_loop(0, heads, over_head, (jnp.int32(0),) * owned)
    for c in range(owned):
        starts[c, heads] = at[c]


def plan(me, ids, counts, tiles, owned, side):
    heads, slots = ids.shape
    query, tile = ids // tiles, ids % tiles
    owner, chunk = query // owned, query % owned
    dx = (me // side - owner // side) % side
    dy = (me % side - owner % side) % side
    head = jnp.arange(heads, dtype=jnp.int32)[:, None]
    position = jnp.where(head < heads // 2, dy * side + dx, dx * side + dy)
    codes = (((chunk * 16 + head) * 256 + owner) * 256 + position) * 256 + tile
    smem = pl.BlockSpec(memory_space=pltpu.SMEM)
    return pl.pallas_call(
        functools.partial(plan_kernel, owned),
        out_shape=(
            jax.ShapeDtypeStruct((owned, heads * slots + PLAN_UNROLL), jnp.int32),
            jax.ShapeDtypeStruct((owned, heads + 1), jnp.int32),
        ),
        in_specs=[smem, smem],
        out_specs=(smem, smem),
        compiler_params=pltpu.CompilerParams(vmem_limit_bytes=1024 * 1024),
        name="plan",
    )(codes, counts)


def regroup_kernel(side, *refs):
    pieces, lines = refs[: 2 * side], refs[2 * side :]
    for n, line in enumerate(lines):
        chunk, half = divmod(n, 2)
        for d in range(side):
            piece = pieces[half * side + d]
            line[d * BLOCK : (d + 1) * BLOCK] = piece[chunk * BLOCK : (chunk + 1) * BLOCK]


def regroup(halves, side, owned):
    vmem = pl.BlockSpec(memory_space=pltpu.VMEM)
    line = jax.ShapeDtypeStruct((side * BLOCK, halves[0].shape[1]), BF16)
    lines = pl.pallas_call(
        functools.partial(regroup_kernel, side),
        out_shape=[line] * (2 * owned),
        in_specs=[vmem] * (2 * side),
        out_specs=[vmem] * (2 * owned),
        compiler_params=pltpu.CompilerParams(vmem_limit_bytes=8 * 1024 * 1024),
        name="regroup",
    )(*halves)
    return [(lines[2 * c], lines[2 * c + 1]) for c in range(owned)]


def attend_kernel(chunk, sources, entries, starts, *refs):
    blocks = 1 + max(i for pieces in sources for i, _ in pieces)
    q_hbm = refs[:blocks]
    k_hbm, v_hbm, out_ref, qs, ks, vs, acc, top, den, stats, sems = refs[blocks:]
    heads, owners, _, width = qs.shape
    scale = width**-0.5 * math.log2(math.e)

    def copies(h):
        moves = [(k_hbm.at[:, h * width : (h + 1) * width], ks.at[h])]
        moves.append((v_hbm.at[:, h * width : (h + 1) * width], vs.at[h]))
        for n, (i, lane) in enumerate(sources[h]):
            blocks = q_hbm[i].shape[0]
            src = q_hbm[i].at[:, :, lane * width : (lane + 1) * width]
            moves.append((src, qs.at[h, n * blocks : (n + 1) * blocks]))
        return [
            pltpu.make_async_copy(src, dst, sems.at[h, i]) for i, (src, dst) in enumerate(moves)
        ]

    for h in range(heads):
        for copy in copies(h):
            copy.start()
    acc[...] = jnp.zeros_like(acc)
    den[...] = jnp.zeros_like(den)
    top[...] = jnp.full_like(top, -jnp.inf)
    count = starts[chunk, heads]
    groups = lax.div(count + UNROLL - 1, jnp.int32(UNROLL))
    opens = [lax.div(starts[chunk, h], jnp.int32(UNROLL)) for h in range(heads)]

    def group(step, carry):
        for h in range(heads):

            @pl.when(step == opens[h])
            def _():
                for copy in copies(h):
                    copy.wait()

        slots = []
        for u in range(UNROLL):
            j = step * UNROLL + u
            live = j < count
            entry = jnp.where(live, entries[chunk, j], 0)
            head = lax.bitwise_and(lax.shift_right_logical(entry, 24), 15)
            owner = lax.bitwise_and(lax.shift_right_logical(entry, 16), 255)
            position = lax.bitwise_and(lax.shift_right_logical(entry, 8), 255)
            tile = lax.bitwise_and(entry, 255)
            slot = jnp.where(live, head * owners + owner, heads * owners)
            slots.append((slot, head, position, tile))

        def rows(i):
            return pl.ds(pl.multiple_of(i * BLOCK, BLOCK), BLOCK)

        scores = [
            lax.dot_general(
                ks[head, rows(tile), :],
                qs[head, position],
                (((1,), (1,)), ((), ())),
                preferred_element_type=F32,
            )
            for _, head, position, tile in slots
        ]
        scores = [s * scale for s in scores]
        tops = [jnp.max(s, axis=0, keepdims=True) for s in scores]
        steps = []
        for (slot, _, _, _), m in zip(slots, tops):
            row = pl.ds(slot, 1)
            old = top[row, :]
            new = jnp.maximum(old, m)
            top[row, :] = new
            steps.append((new, jnp.exp2(old - new)))
        parts = []
        for (slot, head, _, tile), s, (new, _) in zip(slots, scores, steps):
            p = jnp.exp2(s - new)
            d = jnp.sum(p, axis=0, keepdims=True)
            o = lax.dot_general(
                vs[head, rows(tile), :],
                p.astype(BF16),
                (((0,), (0,)), ((), ())),
                preferred_element_type=F32,
            )
            parts.append((d, o))
        for (slot, _, _, _), (_, keep), (d, o) in zip(slots, steps, parts):
            row = pl.ds(slot, 1)
            den[row, :] = den[row, :] * keep + d
            acc[slot] = acc[slot] * keep + o
        return carry

    lax.fori_loop(0, groups, group, 0)
    for h in range(heads):

        @pl.when(opens[h] >= groups)
        def _():
            for copy in copies(h):
                copy.wait()

    used = heads * owners
    total = den[0:used, :]
    listed = total > 0
    safe = jnp.where(listed, total, 1.0)
    level = jnp.where(listed, top[0:used, :] + jnp.log2(safe), ABSENT)
    den[0:used, :] = jnp.where(listed, 1.0 / safe, 0.0)
    for h in range(heads):
        for q in range(owners):
            at = h * owners + q
            out_ref[q, h * width : (h + 1) * width, :] = (acc[at] * den[at : at + 1, :]).astype(BF16)
        for i, piece in enumerate(split3(level[h * owners : (h + 1) * owners])):
            stats[3 * h + i] = piece
    first = out_ref.shape[1] - STAT_ROWS
    for q in range(owners):
        rows = [stats[i, q : q + 1, :] for i in range(3 * heads)]
        rows.append(jnp.zeros((STAT_ROWS - 3 * heads, BLOCK), F32))
        out_ref[q, first:, :] = jnp.concatenate(rows, axis=0).astype(BF16)


def in_hbm(x):
    return pltpu.with_memory_space_constraint(x, pltpu.HBM)


def attend(chunk, entries, starts, queries, sources, keys, values):
    heads = len(sources)
    width = keys.shape[1] // heads
    owners = sum(queries[i].shape[0] for i, _ in sources[0])
    smem = pl.BlockSpec(memory_space=pltpu.SMEM)
    hbm = pl.BlockSpec(memory_space=pl.ANY)
    lines = -(-(heads * owners + 1) // 8) * 8
    return pl.pallas_call(
        functools.partial(attend_kernel, chunk, sources),
        out_shape=jax.ShapeDtypeStruct((owners, heads * width + STAT_ROWS, BLOCK), BF16),
        in_specs=[smem, smem] + [hbm] * (len(queries) + 2),
        scratch_shapes=[
            pltpu.VMEM((heads, owners, BLOCK, width), BF16),
            pltpu.VMEM((heads, keys.shape[0], width), BF16),
            pltpu.VMEM((heads, values.shape[0], width), BF16),
            pltpu.VMEM((heads * owners + 1, width, BLOCK), F32),
            pltpu.VMEM((lines, BLOCK), F32),
            pltpu.VMEM((lines, BLOCK), F32),
            pltpu.VMEM((3 * heads, owners, BLOCK), F32),
            pltpu.SemaphoreType.DMA((heads, 2 + max(len(p) for p in sources))),
        ],
        compiler_params=pltpu.CompilerParams(vmem_limit_bytes=40 * 1024 * 1024),
        name="attend",
    )(entries, starts, *queries, in_hbm(keys), in_hbm(values))


def project_kernel(heads, core, in_ref, weight, own_ref, other_ref, mixed, held, sems):
    ranges, total, rows = in_ref.shape
    width = (total - STAT_ROWS) // heads
    first = total - STAT_ROWS
    zs, _, span = own_ref.shape

    def copy(z, s):
        column = pl.multiple_of((2 * z + jnp.bitwise_xor(core[0], s)) * span, span)
        return pltpu.make_async_copy(
            weight.at[:, pl.ds(column, span)], held.at[z, s], sems.at[z, s]
        )

    turns = [(z, s) for z in range(zs) for s in range(2)]
    for z, s in turns:
        copy(z, s).start()
    stats = in_ref[:, first:, :].astype(F32)
    for h in range(heads):
        level = stats[:, 3 * h, :] + stats[:, 3 * h + 1, :] + stats[:, 3 * h + 2, :]
        share = jnp.exp2(level - jnp.max(level, axis=0, keepdims=True))
        share = share / jnp.sum(share, axis=0, keepdims=True)
        acc = jnp.zeros((width, rows), F32)
        for r in range(ranges):
            acc += in_ref[r, h * width : (h + 1) * width, :].astype(F32) * share[r : r + 1, :]
        mixed[h * width : (h + 1) * width, :] = acc.astype(BF16)
    for z, s in turns:
        copy(z, s).wait()
        (own_ref, other_ref)[s][z] = lax.dot_general(
            mixed[...], held[z, s], (((0,), (0,)), ((), ())), preferred_element_type=F32
        ).astype(BF16)


def project(core, parts, weight, heads, span):
    depth = weight.shape[0]
    zs = weight.shape[1] // span // 2
    rows = parts.shape[2]
    result = pl.BlockSpec((zs, rows, span), lambda i, core: (0, 0, 0))
    return pl.pallas_call(
        functools.partial(project_kernel, heads),
        out_shape=[jax.ShapeDtypeStruct((zs, rows, span), BF16)] * 2,
        grid_spec=pltpu.PrefetchScalarGridSpec(
            num_scalar_prefetch=1,
            grid=(1,),
            in_specs=[
                pl.BlockSpec(parts.shape, lambda i, core: (0, 0, 0)),
                pl.BlockSpec(memory_space=pl.ANY),
            ],
            out_specs=[result, result],
            scratch_shapes=[
                pltpu.VMEM((depth, rows), BF16),
                pltpu.VMEM((zs, 2, depth, span), BF16),
                pltpu.SemaphoreType.DMA((zs, 2)),
            ],
        ),
        compiler_params=pltpu.CompilerParams(vmem_limit_bytes=14 * 1024 * 1024),
        name="project",
    )(core, parts, in_hbm(weight))


def pair_kernel(z, mine, theirs, own, *others):
    zs = mine.shape[0]
    for d, out in zip((0,) + Z_STEPS, (own,) + others):
        at = lax.rem(z[0] + d, jnp.int32(zs))
        out[...] = (mine[at].astype(F32) + theirs[at].astype(F32)).astype(out.dtype)


def pair(z, mine, theirs):
    shape = mine.shape[1:]
    whole = pl.BlockSpec(mine.shape, lambda i, z: (0, 0, 0))
    return pl.pallas_call(
        pair_kernel,
        out_shape=[jax.ShapeDtypeStruct(shape, F32)]
        + [jax.ShapeDtypeStruct(shape, BF16) for _ in Z_STEPS],
        grid_spec=pltpu.PrefetchScalarGridSpec(
            num_scalar_prefetch=1,
            grid=(1,),
            in_specs=[whole, whole],
            out_specs=[pl.BlockSpec(shape, lambda i, z: (0, 0))] * (1 + len(Z_STEPS)),
        ),
        compiler_params=pltpu.CompilerParams(vmem_limit_bytes=8 * 1024 * 1024),
        name="pair",
    )(z, mine, theirs)


def local(queries, key_states, value_states, block_ids, block_counts, out_weight):
    heads = block_ids.shape[0]
    ranges = lax.axis_size("keys")
    groups = lax.axis_size("heads")
    me = lax.axis_index("heads")
    core = jnp.reshape(me % 2, (1,)).astype(jnp.int32)
    z = jnp.reshape(me // 2, (1,)).astype(jnp.int32)
    span = out_weight.shape[1] // groups
    tiles = key_states.shape[0] // BLOCK
    owned = queries.shape[0] // BLOCK
    side = math.isqrt(ranges)

    def exchange(parts):
        return lax.all_to_all(parts, "keys", split_axis=0, concat_axis=0, tiled=True)

    def finish(got):
        mine, theirs = project(core, got, out_weight, heads, span)
        swap = [(g, g ^ 1) for g in range(groups)]
        own, *others = pair(z, mine, lax.ppermute(theirs, "heads", swap))
        total = own
        for d, piece in zip(Z_STEPS, others):
            pairs = [(g, (g + 2 * d) % groups) for g in range(groups)]
            total = total + lax.ppermute(piece, "heads", pairs).astype(F32)
        return total.astype(BF16)

    def along(x, axis):
        def pairs(d):
            there = lambda i, j: ((i + d) % side, j) if axis == 0 else (i, (j + d) % side)
            moved = [there(k // side, k % side) for k in range(ranges)]
            return [(k, i * side + j) for k, (i, j) in enumerate(moved)]

        return {d: lax.ppermute(x, "keys", pairs(d)) for d in Z_STEPS}

    def line(x, got):
        return [x] + [got[d] for d in range(1, side)]

    middle = queries.shape[1] // 2
    left, right = queries[:, :middle], queries[:, middle:]
    left, right = lax.optimization_barrier((left, right))
    halves = line(left, along(left, 0)) + line(right, along(right, 1))
    halves = lax.optimization_barrier(halves)
    far = max(Z_STEPS, key=lambda d: min(d, side - d))
    ready, later = [], []
    for c, (left, right) in enumerate(regroup(halves, side, owned)):
        left, right = lax.optimization_barrier((left, right))
        got = [along(left, 1), along(right, 0)]
        later.append((left, right, got))
        if c == 0:
            ready += [g[d] for g in got for d in Z_STEPS]
        else:
            ready += [g[far] for g in got]
    ready = iter(lax.optimization_barrier(ready))
    for c, (_, _, got) in enumerate(later):
        for g in got:
            g.update({d: next(ready) for d in (Z_STEPS if c == 0 else (far,))})

    def source(c):
        left, right, (up, across) = later[c]
        pieces = line(left, up) + line(right, across)
        return [x.reshape(side, BLOCK, middle) for x in pieces]

    lower = [[(i, h) for i in range(side)] for h in range(heads // 2)]
    upper = [[(side + i, h) for i in range(side)] for h in range(heads // 2)]

    slot = jnp.reshape(lax.axis_index("keys"), (1,)).astype(jnp.int32)
    entries, starts = plan(slot, block_ids, block_counts, tiles, owned, side)
    outs = []
    for c in range(owned):
        parts = attend(c, entries, starts, source(c), lower + upper, key_states, value_states)
        if c == 0:
            near = [g[d] for _, _, got in later[1:] for g in got for d in Z_STEPS if d != far]
            parts, *near = lax.optimization_barrier([parts] + near)
            near = iter(near)
            for _, _, got in later[1:]:
                for g in got:
                    g.update({d: next(near) for d in Z_STEPS if d != far})
        got = exchange(parts)
        if outs:
            got, outs[-1] = lax.optimization_barrier((got, outs[-1]))
        outs.append(finish(got))
    return jnp.concatenate(outs)


def solution(mesh):
    in_specs = (
        P("keys", "heads"),
        P("keys", "heads"),
        P("keys", "heads"),
        P("heads", "keys"),
        P("heads", "keys"),
        P("heads", None),
    )
    return jax.shard_map(
        local, mesh=mesh, in_specs=in_specs, out_specs=P("keys", "heads"), check_vma=False
    )
```

```python
import functools
import math

import jax
import jax.numpy as jnp
from jax import lax
from jax.experimental import pallas as pl
from jax.experimental.pallas import tpu as pltpu
from jax.sharding import PartitionSpec as P

BLOCK = 128
UNROLL = 16
PLAN_UNROLL = 8
CHUNK_BIT = 28
STAT_ROWS = 16
ABSENT = -3.0e38
Z_STEPS = (1, 3, 2)
F32 = jnp.float32
BF16 = jnp.bfloat16


def split3(x):
    high = x.astype(BF16).astype(F32)
    rest = x - high
    middle = rest.astype(BF16).astype(F32)
    return high, middle, rest - middle


def plan_kernel(owned, codes, counts, entries, starts):
    heads = codes.shape[0]

    def over_head(h, at):
        for c in range(owned):
            starts[c, h] = at[c]
        count = counts[h, 0]

        def some(step, at):
            for u in range(PLAN_UNROLL):
                j = step * PLAN_UNROLL + u
                code = codes[h, j]
                chunk = lax.shift_right_logical(code, CHUNK_BIT)
                place = at[0]
                for c in range(1, owned):
                    place = jnp.where(chunk == c, at[c], place)
                entries[chunk, place] = code
                live = j < count
                at = tuple(
                    a + jnp.where(live & (chunk == c), 1, 0) for c, a in enumerate(at)
                )
            return at

        return lax.fori_loop(0, lax.div(count + PLAN_UNROLL - 1, PLAN_UNROLL), some, at)

    at = lax.fori_loop(0, heads, over_head, (jnp.int32(0),) * owned)
    for c in range(owned):
        starts[c, heads] = at[c]


def plan(me, ids, counts, tiles, owned, side):
    heads, slots = ids.shape
    query, tile = ids // tiles, ids % tiles
    owner, chunk = query // owned, query % owned
    dx = (me // side - owner // side) % side
    dy = (me % side - owner % side) % side
    head = jnp.arange(heads, dtype=jnp.int32)[:, None]
    position = jnp.where(head < heads // 2, dy * side + dx, dx * side + dy)
    codes = (((chunk * 16 + head) * 256 + owner) * 256 + position) * 256 + tile
    smem = pl.BlockSpec(memory_space=pltpu.SMEM)
    return pl.pallas_call(
        functools.partial(plan_kernel, owned),
        out_shape=(
            jax.ShapeDtypeStruct((owned, heads * slots + PLAN_UNROLL), jnp.int32),
            jax.ShapeDtypeStruct((owned, heads + 1), jnp.int32),
        ),
        in_specs=[smem, smem],
        out_specs=(smem, smem),
        compiler_params=pltpu.CompilerParams(vmem_limit_bytes=1024 * 1024),
        name="plan",
    )(codes, counts)


def regroup_kernel(side, *refs):
    pieces, lines, everything = refs[: 2 * side], refs[2 * side : -2], refs[-2:]
    for n, line in enumerate(lines):
        chunk, half = divmod(n, 2)
        for d in range(side):
            piece = pieces[half * side + d][chunk * BLOCK : (chunk + 1) * BLOCK]
            line[d] = piece
            everything[half][chunk, d] = piece


def regroup(halves, side, owned):
    vmem = pl.BlockSpec(memory_space=pltpu.VMEM)
    shape = (side, BLOCK, halves[0].shape[1])
    line = jax.ShapeDtypeStruct(shape, BF16)
    whole = jax.ShapeDtypeStruct((owned,) + shape, BF16)
    out = pl.pallas_call(
        functools.partial(regroup_kernel, side),
        out_shape=[line] * (2 * owned) + [whole] * 2,
        in_specs=[vmem] * (2 * side),
        out_specs=[vmem] * (2 * owned + 2),
        compiler_params=pltpu.CompilerParams(vmem_limit_bytes=8 * 1024 * 1024),
        name="regroup",
    )(*halves)
    return [(out[2 * c], out[2 * c + 1]) for c in range(owned)], out[-2:]


def attend_kernel(chunk, sources, entries, starts, *refs):
    blocks = 1 + max(i for pieces in sources for i, _ in pieces)
    q_hbm = refs[:blocks]
    k_hbm, v_hbm, out_ref, qs, ks, vs, acc, top, den, stats, sems = refs[blocks:]
    heads, owners, _, width = qs.shape
    scale = width**-0.5 * math.log2(math.e)

    def copies(h):
        moves = [(k_hbm.at[:, h * width : (h + 1) * width], ks.at[h])]
        moves.append((v_hbm.at[:, h * width : (h + 1) * width], vs.at[h]))
        for n, (i, lane) in enumerate(sources[h]):
            blocks = q_hbm[i].shape[-3]
            held = q_hbm[i].at[chunk] if len(q_hbm[i].shape) == 4 else q_hbm[i]
            src = held.at[:, :, lane * width : (lane + 1) * width]
            moves.append((src, qs.at[h, n * blocks : (n + 1) * blocks]))
        return [
            pltpu.make_async_copy(src, dst, sems.at[h, i]) for i, (src, dst) in enumerate(moves)
        ]

    for h in range(heads):
        for copy in copies(h):
            copy.start()
    acc[...] = jnp.zeros_like(acc)
    den[...] = jnp.zeros_like(den)
    top[...] = jnp.full_like(top, -jnp.inf)
    count = starts[chunk, heads]
    groups = lax.div(count + UNROLL - 1, jnp.int32(UNROLL))
    opens = [lax.div(starts[chunk, h], jnp.int32(UNROLL)) for h in range(heads)]

    def group(step, carry):
        for h in range(heads):

            @pl.when(step == opens[h])
            def _():
                for copy in copies(h):
                    copy.wait()

        slots = []
        for u in range(UNROLL):
            j = step * UNROLL + u
            live = j < count
            entry = jnp.where(live, entries[chunk, j], 0)
            head = lax.bitwise_and(lax.shift_right_logical(entry, 24), 15)
            owner = lax.bitwise_and(lax.shift_right_logical(entry, 16), 255)
            position = lax.bitwise_and(lax.shift_right_logical(entry, 8), 255)
            tile = lax.bitwise_and(entry, 255)
            slot = jnp.where(live, head * owners + owner, heads * owners)
            slots.append((slot, head, position, tile))

        def rows(i):
            return pl.ds(pl.multiple_of(i * BLOCK, BLOCK), BLOCK)

        scores = [
            lax.dot_general(
                ks[head, rows(tile), :],
                qs[head, position],
                (((1,), (1,)), ((), ())),
                preferred_element_type=F32,
            )
            for _, head, position, tile in slots
        ]
        scores = [s * scale for s in scores]
        tops = [jnp.max(s, axis=0, keepdims=True) for s in scores]
        steps = []
        for (slot, _, _, _), m in zip(slots, tops):
            row = pl.ds(slot, 1)
            old = top[row, :]
            new = jnp.maximum(old, m)
            top[row, :] = new
            steps.append((new, jnp.exp2(old - new)))
        parts = []
        for (slot, head, _, tile), s, (new, _) in zip(slots, scores, steps):
            p = jnp.exp2(s - new)
            d = jnp.sum(p, axis=0, keepdims=True)
            o = lax.dot_general(
                vs[head, rows(tile), :],
                p.astype(BF16),
                (((0,), (0,)), ((), ())),
                preferred_element_type=F32,
            )
            parts.append((d, o))
        for (slot, _, _, _), (_, keep), (d, o) in zip(slots, steps, parts):
            row = pl.ds(slot, 1)
            den[row, :] = den[row, :] * keep + d
            acc[slot] = acc[slot] * keep + o
        return carry

    lax.fori_loop(0, groups, group, 0)
    for h in range(heads):

        @pl.when(opens[h] >= groups)
        def _():
            for copy in copies(h):
                copy.wait()

    used = heads * owners
    total = den[0:used, :]
    listed = total > 0
    safe = jnp.where(listed, total, 1.0)
    level = jnp.where(listed, top[0:used, :] + jnp.log2(safe), ABSENT)
    den[0:used, :] = jnp.where(listed, 1.0 / safe, 0.0)
    for h in range(heads):
        for q in range(owners):
            at = h * owners + q
            out_ref[q, h * width : (h + 1) * width, :] = (acc[at] * den[at : at + 1, :]).astype(BF16)
        for i, piece in enumerate(split3(level[h * owners : (h + 1) * owners])):
            stats[3 * h + i] = piece
    first = out_ref.shape[1] - STAT_ROWS
    for q in range(owners):
        rows = [stats[i, q : q + 1, :] for i in range(3 * heads)]
        rows.append(jnp.zeros((STAT_ROWS - 3 * heads, BLOCK), F32))
        out_ref[q, first:, :] = jnp.concatenate(rows, axis=0).astype(BF16)


def in_hbm(x):
    return pltpu.with_memory_space_constraint(x, pltpu.HBM)


def attend(chunk, entries, starts, queries, sources, keys, values):
    heads = len(sources)
    width = keys.shape[1] // heads
    owners = sum(queries[i].shape[-3] for i, _ in sources[0])
    smem = pl.BlockSpec(memory_space=pltpu.SMEM)
    hbm = pl.BlockSpec(memory_space=pl.ANY)
    lines = -(-(heads * owners + 1) // 8) * 8
    return pl.pallas_call(
        functools.partial(attend_kernel, chunk, sources),
        out_shape=jax.ShapeDtypeStruct((owners, heads * width + STAT_ROWS, BLOCK), BF16),
        in_specs=[smem, smem] + [hbm] * (len(queries) + 2),
        scratch_shapes=[
            pltpu.VMEM((heads, owners, BLOCK, width), BF16),
            pltpu.VMEM((heads, keys.shape[0], width), BF16),
            pltpu.VMEM((heads, values.shape[0], width), BF16),
            pltpu.VMEM((heads * owners + 1, width, BLOCK), F32),
            pltpu.VMEM((lines, BLOCK), F32),
            pltpu.VMEM((lines, BLOCK), F32),
            pltpu.VMEM((3 * heads, owners, BLOCK), F32),
            pltpu.SemaphoreType.DMA((heads, 2 + max(len(p) for p in sources))),
        ],
        compiler_params=pltpu.CompilerParams(vmem_limit_bytes=40 * 1024 * 1024),
        name="attend",
    )(entries, starts, *queries, in_hbm(keys), in_hbm(values))


def project_kernel(heads, core, in_ref, weight, own_ref, other_ref, mixed, held, sems):
    ranges, total, rows = in_ref.shape
    width = (total - STAT_ROWS) // heads
    first = total - STAT_ROWS
    zs, _, span = own_ref.shape

    def copy(z, s):
        column = pl.multiple_of((2 * z + jnp.bitwise_xor(core[0], s)) * span, span)
        return pltpu.make_async_copy(
            weight.at[:, pl.ds(column, span)], held.at[z, s], sems.at[z, s]
        )

    turns = [(z, s) for z in range(zs) for s in range(2)]
    for z, s in turns:
        copy(z, s).start()
    stats = in_ref[:, first:, :].astype(F32)
    for h in range(heads):
        level = stats[:, 3 * h, :] + stats[:, 3 * h + 1, :] + stats[:, 3 * h + 2, :]
        share = jnp.exp2(level - jnp.max(level, axis=0, keepdims=True))
        share = share / jnp.sum(share, axis=0, keepdims=True)
        acc = jnp.zeros((width, rows), F32)
        for r in range(ranges):
            acc += in_ref[r, h * width : (h + 1) * width, :].astype(F32) * share[r : r + 1, :]
        mixed[h * width : (h + 1) * width, :] = acc.astype(BF16)
    for z, s in turns:
        copy(z, s).wait()
        (own_ref, other_ref)[s][z] = lax.dot_general(
            mixed[...], held[z, s], (((0,), (0,)), ((), ())), preferred_element_type=F32
        ).astype(BF16)


def project(core, parts, weight, heads, span):
    depth = weight.shape[0]
    zs = weight.shape[1] // span // 2
    rows = parts.shape[2]
    result = pl.BlockSpec((zs, rows, span), lambda i, core: (0, 0, 0))
    return pl.pallas_call(
        functools.partial(project_kernel, heads),
        out_shape=[jax.ShapeDtypeStruct((zs, rows, span), BF16)] * 2,
        grid_spec=pltpu.PrefetchScalarGridSpec(
            num_scalar_prefetch=1,
            grid=(1,),
            in_specs=[
                pl.BlockSpec(parts.shape, lambda i, core: (0, 0, 0)),
                pl.BlockSpec(memory_space=pl.ANY),
            ],
            out_specs=[result, result],
            scratch_shapes=[
                pltpu.VMEM((depth, rows), BF16),
                pltpu.VMEM((zs, 2, depth, span), BF16),
                pltpu.SemaphoreType.DMA((zs, 2)),
            ],
        ),
        compiler_params=pltpu.CompilerParams(vmem_limit_bytes=14 * 1024 * 1024),
        name="project",
    )(core, parts, in_hbm(weight))


def pair_kernel(z, mine, theirs, own, *others):
    zs = mine.shape[0]
    for d, out in zip((0,) + Z_STEPS, (own,) + others):
        at = lax.rem(z[0] + d, jnp.int32(zs))
        out[...] = (mine[at].astype(F32) + theirs[at].astype(F32)).astype(out.dtype)


def pair(z, mine, theirs):
    shape = mine.shape[1:]
    whole = pl.BlockSpec(mine.shape, lambda i, z: (0, 0, 0))
    return pl.pallas_call(
        pair_kernel,
        out_shape=[jax.ShapeDtypeStruct(shape, F32)]
        + [jax.ShapeDtypeStruct(shape, BF16) for _ in Z_STEPS],
        grid_spec=pltpu.PrefetchScalarGridSpec(
            num_scalar_prefetch=1,
            grid=(1,),
            in_specs=[whole, whole],
            out_specs=[pl.BlockSpec(shape, lambda i, z: (0, 0))] * (1 + len(Z_STEPS)),
        ),
        compiler_params=pltpu.CompilerParams(vmem_limit_bytes=8 * 1024 * 1024),
        name="pair",
    )(z, mine, theirs)


def local(queries, key_states, value_states, block_ids, block_counts, out_weight):
    heads = block_ids.shape[0]
    ranges = lax.axis_size("keys")
    groups = lax.axis_size("heads")
    me = lax.axis_index("heads")
    core = jnp.reshape(me % 2, (1,)).astype(jnp.int32)
    z = jnp.reshape(me // 2, (1,)).astype(jnp.int32)
    span = out_weight.shape[1] // groups
    tiles = key_states.shape[0] // BLOCK
    owned = queries.shape[0] // BLOCK
    side = math.isqrt(ranges)

    def exchange(parts):
        return lax.all_to_all(parts, "keys", split_axis=0, concat_axis=0, tiled=True)

    def finish(got):
        mine, theirs = project(core, got, out_weight, heads, span)
        swap = [(g, g ^ 1) for g in range(groups)]
        own, *others = pair(z, mine, lax.ppermute(theirs, "heads", swap))
        total = own
        for d, piece in zip(Z_STEPS, others):
            pairs = [(g, (g + 2 * d) % groups) for g in range(groups)]
            total = total + lax.ppermute(piece, "heads", pairs).astype(F32)
        return total.astype(BF16)

    def along(x, axis):
        def pairs(d):
            there = lambda i, j: ((i + d) % side, j) if axis == 0 else (i, (j + d) % side)
            moved = [there(k // side, k % side) for k in range(ranges)]
            return [(k, i * side + j) for k, (i, j) in enumerate(moved)]

        return lambda d: lax.ppermute(x, "keys", pairs(d))

    def line(x, get):
        got = {d: get(d) for d in Z_STEPS}
        return [x] + [got[d] for d in range(1, side)]

    middle = queries.shape[1] // 2
    left, right = queries[:, :middle], queries[:, middle:]
    left, right = lax.optimization_barrier((left, right))
    halves = line(left, along(left, 0)) + line(right, along(right, 1))
    slot = jnp.reshape(lax.axis_index("keys"), (1,)).astype(jnp.int32)
    entries, starts = plan(slot, block_ids, block_counts, tiles, owned, side)
    *halves, entries, starts = lax.optimization_barrier(halves + [entries, starts])
    chunks, both = lax.optimization_barrier(regroup(halves, side, owned))
    far = max(Z_STEPS, key=lambda d: min(d, side - d))
    near = [d for d in Z_STEPS if d != far]
    axes = (1, 0)
    first = [[along(x, axis)(d) for d in near] for x, axis in zip(chunks[0], axes)]
    beyond = [along(x, axis)(far) for x, axis in zip(both, axes)]
    first, beyond = lax.optimization_barrier((first, beyond))
    rest = [
        [[along(x, axis)(d) for d in near] for x, axis in zip(chunk, axes)] for chunk in chunks[1:]
    ]

    def source(own, got):
        pieces = []
        for half in range(2):
            found = dict(zip(near, got[half]))
            found[far] = beyond[half]
            pieces += [own[half]] + [found[d] for d in range(1, side)]
        return pieces

    lower = [[(i, h) for i in range(side)] for h in range(heads // 2)]
    upper = [[(side + i, h) for i in range(side)] for h in range(heads // 2)]

    outs = []
    for c in range(owned):
        pieces = source(chunks[c], first if c == 0 else rest[c - 1])
        parts = attend(c, entries, starts, pieces, lower + upper, key_states, value_states)
        if c == 0:
            parts, rest = lax.optimization_barrier((parts, rest))
            rest = jax.tree.map(in_hbm, rest)
        got = exchange(parts)
        if outs:
            got, outs[-1] = lax.optimization_barrier((got, outs[-1]))
        outs.append(finish(got))
    return jnp.concatenate(outs)


def solution(mesh):
    in_specs = (
        P("keys", "heads"),
        P("keys", "heads"),
        P("keys", "heads"),
        P("heads", "keys"),
        P("heads", "keys"),
        P("heads", None),
    )
    return jax.shard_map(
        local, mesh=mesh, in_specs=in_specs, out_specs=P("keys", "heads"), check_vma=False
    )
```

```python
import functools
import math

import jax
import jax.numpy as jnp
from jax import lax
from jax.experimental import pallas as pl
from jax.experimental.pallas import tpu as pltpu
from jax.sharding import PartitionSpec as P

BLOCK = 128
UNROLL = 16
PLAN_UNROLL = 8
CHUNK_BIT = 28
STAT_ROWS = 16
ABSENT = -3.0e38
Z_STEPS = (1, 3, 2)
F32 = jnp.float32
BF16 = jnp.bfloat16


def split3(x):
    high = x.astype(BF16).astype(F32)
    rest = x - high
    middle = rest.astype(BF16).astype(F32)
    return high, middle, rest - middle


def plan_kernel(owned, codes, counts, entries, starts):
    heads = codes.shape[0]

    def over_head(h, at):
        for c in range(owned):
            starts[c, h] = at[c]
        count = counts[h, 0]

        def some(step, at):
            for u in range(PLAN_UNROLL):
                j = step * PLAN_UNROLL + u
                code = codes[h, j]
                chunk = lax.shift_right_logical(code, CHUNK_BIT)
                place = at[0]
                for c in range(1, owned):
                    place = jnp.where(chunk == c, at[c], place)
                entries[chunk, place] = code
                live = j < count
                at = tuple(
                    a + jnp.where(live & (chunk == c), 1, 0) for c, a in enumerate(at)
                )
            return at

        return lax.fori_loop(0, lax.div(count + PLAN_UNROLL - 1, PLAN_UNROLL), some, at)

    at = lax.fori_loop(0, heads, over_head, (jnp.int32(0),) * owned)
    for c in range(owned):
        starts[c, heads] = at[c]


def plan(me, ids, counts, tiles, owned, side):
    heads, slots = ids.shape
    query, tile = ids // tiles, ids % tiles
    owner, chunk = query // owned, query % owned
    dx = (me // side - owner // side) % side
    dy = (me % side - owner % side) % side
    head = jnp.arange(heads, dtype=jnp.int32)[:, None]
    position = jnp.where(head < heads // 2, dy * side + dx, dx * side + dy)
    codes = (((chunk * 16 + head) * 256 + owner) * 256 + position) * 256 + tile
    smem = pl.BlockSpec(memory_space=pltpu.SMEM)
    return pl.pallas_call(
        functools.partial(plan_kernel, owned),
        out_shape=(
            jax.ShapeDtypeStruct((owned, heads * slots + PLAN_UNROLL), jnp.int32),
            jax.ShapeDtypeStruct((owned, heads + 1), jnp.int32),
        ),
        in_specs=[smem, smem],
        out_specs=(smem, smem),
        compiler_params=pltpu.CompilerParams(vmem_limit_bytes=1024 * 1024),
        name="plan",
    )(codes, counts)


def regroup_kernel(side, *refs):
    pieces, lines = refs[: 2 * side], refs[2 * side :]
    for n, line in enumerate(lines):
        chunk, half = divmod(n, 2)
        for d in range(side):
            piece = pieces[half * side + d]
            line[d * BLOCK : (d + 1) * BLOCK] = piece[chunk * BLOCK : (chunk + 1) * BLOCK]


def regroup(halves, side, owned):
    vmem = pl.BlockSpec(memory_space=pltpu.VMEM)
    line = jax.ShapeDtypeStruct((side * BLOCK, halves[0].shape[1]), BF16)
    lines = pl.pallas_call(
        functools.partial(regroup_kernel, side),
        out_shape=[line] * (2 * owned),
        in_specs=[vmem] * (2 * side),
        out_specs=[vmem] * (2 * owned),
        compiler_params=pltpu.CompilerParams(vmem_limit_bytes=8 * 1024 * 1024),
        name="regroup",
    )(*halves)
    return [(lines[2 * c], lines[2 * c + 1]) for c in range(owned)]


def attend_kernel(chunk, sources, entries, starts, *refs):
    blocks = 1 + max(i for pieces in sources for i, _ in pieces)
    q_hbm = refs[:blocks]
    k_hbm, v_hbm, out_ref, qs, ks, vs, acc, top, den, stats, sems = refs[blocks:]
    heads, owners, _, width = qs.shape
    scale = width**-0.5 * math.log2(math.e)

    def copies(h):
        moves = [(k_hbm.at[:, h * width : (h + 1) * width], ks.at[h])]
        moves.append((v_hbm.at[:, h * width : (h + 1) * width], vs.at[h]))
        for n, (i, lane) in enumerate(sources[h]):
            blocks = q_hbm[i].shape[0]
            src = q_hbm[i].at[:, :, lane * width : (lane + 1) * width]
            moves.append((src, qs.at[h, n * blocks : (n + 1) * blocks]))
        return [
            pltpu.make_async_copy(src, dst, sems.at[h, i]) for i, (src, dst) in enumerate(moves)
        ]

    for h in range(heads):
        for copy in copies(h):
            copy.start()
    acc[...] = jnp.zeros_like(acc)
    den[...] = jnp.zeros_like(den)
    top[...] = jnp.full_like(top, -jnp.inf)
    count = starts[chunk, heads]
    groups = lax.div(count + UNROLL - 1, jnp.int32(UNROLL))
    opens = [lax.div(starts[chunk, h], jnp.int32(UNROLL)) for h in range(heads)]

    def group(step, carry):
        for h in range(heads):

            @pl.when(step == opens[h])
            def _():
                for copy in copies(h):
                    copy.wait()

        slots = []
        for u in range(UNROLL):
            j = step * UNROLL + u
            live = j < count
            entry = jnp.where(live, entries[chunk, j], 0)
            head = lax.bitwise_and(lax.shift_right_logical(entry, 24), 15)
            owner = lax.bitwise_and(lax.shift_right_logical(entry, 16), 255)
            position = lax.bitwise_and(lax.shift_right_logical(entry, 8), 255)
            tile = lax.bitwise_and(entry, 255)
            slot = jnp.where(live, head * owners + owner, heads * owners)
            slots.append((slot, head, position, tile))

        def rows(i):
            return pl.ds(pl.multiple_of(i * BLOCK, BLOCK), BLOCK)

        scores = [
            lax.dot_general(
                ks[head, rows(tile), :],
                qs[head, position],
                (((1,), (1,)), ((), ())),
                preferred_element_type=F32,
            )
            for _, head, position, tile in slots
        ]
        scores = [s * scale for s in scores]
        tops = [jnp.max(s, axis=0, keepdims=True) for s in scores]
        steps = []
        for (slot, _, _, _), m in zip(slots, tops):
            row = pl.ds(slot, 1)
            old = top[row, :]
            new = jnp.maximum(old, m)
            top[row, :] = new
            steps.append((new, jnp.exp2(old - new)))
        parts = []
        for (slot, head, _, tile), s, (new, _) in zip(slots, scores, steps):
            p = jnp.exp2(s - new)
            d = jnp.sum(p, axis=0, keepdims=True)
            o = lax.dot_general(
                vs[head, rows(tile), :],
                p.astype(BF16),
                (((0,), (0,)), ((), ())),
                preferred_element_type=F32,
            )
            parts.append((d, o))
        for (slot, _, _, _), (_, keep), (d, o) in zip(slots, steps, parts):
            row = pl.ds(slot, 1)
            den[row, :] = den[row, :] * keep + d
            acc[slot] = acc[slot] * keep + o
        return carry

    lax.fori_loop(0, groups, group, 0)
    for h in range(heads):

        @pl.when(opens[h] >= groups)
        def _():
            for copy in copies(h):
                copy.wait()

    used = heads * owners
    total = den[0:used, :]
    listed = total > 0
    safe = jnp.where(listed, total, 1.0)
    level = jnp.where(listed, top[0:used, :] + jnp.log2(safe), ABSENT)
    den[0:used, :] = jnp.where(listed, 1.0 / safe, 0.0)
    for h in range(heads):
        for q in range(owners):
            at = h * owners + q
            out_ref[q, h * width : (h + 1) * width, :] = (acc[at] * den[at : at + 1, :]).astype(BF16)
        for i, piece in enumerate(split3(level[h * owners : (h + 1) * owners])):
            stats[3 * h + i] = piece
    first = out_ref.shape[1] - STAT_ROWS
    for q in range(owners):
        rows = [stats[i, q : q + 1, :] for i in range(3 * heads)]
        rows.append(jnp.zeros((STAT_ROWS - 3 * heads, BLOCK), F32))
        out_ref[q, first:, :] = jnp.concatenate(rows, axis=0).astype(BF16)


def in_hbm(x):
    return pltpu.with_memory_space_constraint(x, pltpu.HBM)


def attend(chunk, entries, starts, queries, sources, keys, values):
    heads = len(sources)
    width = keys.shape[1] // heads
    owners = sum(queries[i].shape[0] for i, _ in sources[0])
    smem = pl.BlockSpec(memory_space=pltpu.SMEM)
    hbm = pl.BlockSpec(memory_space=pl.ANY)
    lines = -(-(heads * owners + 1) // 8) * 8
    return pl.pallas_call(
        functools.partial(attend_kernel, chunk, sources),
        out_shape=jax.ShapeDtypeStruct((owners, heads * width + STAT_ROWS, BLOCK), BF16),
        in_specs=[smem, smem] + [hbm] * (len(queries) + 2),
        scratch_shapes=[
            pltpu.VMEM((heads, owners, BLOCK, width), BF16),
            pltpu.VMEM((heads, keys.shape[0], width), BF16),
            pltpu.VMEM((heads, values.shape[0], width), BF16),
            pltpu.VMEM((heads * owners + 1, width, BLOCK), F32),
            pltpu.VMEM((lines, BLOCK), F32),
            pltpu.VMEM((lines, BLOCK), F32),
            pltpu.VMEM((3 * heads, owners, BLOCK), F32),
            pltpu.SemaphoreType.DMA((heads, 2 + max(len(p) for p in sources))),
        ],
        compiler_params=pltpu.CompilerParams(vmem_limit_bytes=40 * 1024 * 1024),
        name="attend",
    )(entries, starts, *queries, in_hbm(keys), in_hbm(values))


def project_kernel(heads, core, in_ref, weight, own_ref, other_ref, mixed, held, sems):
    ranges, total, rows = in_ref.shape
    width = (total - STAT_ROWS) // heads
    first = total - STAT_ROWS
    zs, _, span = own_ref.shape

    def copy(z, s):
        column = pl.multiple_of((2 * z + jnp.bitwise_xor(core[0], s)) * span, span)
        return pltpu.make_async_copy(
            weight.at[:, pl.ds(column, span)], held.at[z, s], sems.at[z, s]
        )

    turns = [(z, s) for z in range(zs) for s in range(2)]
    for z, s in turns:
        copy(z, s).start()
    stats = in_ref[:, first:, :].astype(F32)
    for h in range(heads):
        level = stats[:, 3 * h, :] + stats[:, 3 * h + 1, :] + stats[:, 3 * h + 2, :]
        share = jnp.exp2(level - jnp.max(level, axis=0, keepdims=True))
        share = share / jnp.sum(share, axis=0, keepdims=True)
        acc = jnp.zeros((width, rows), F32)
        for r in range(ranges):
            acc += in_ref[r, h * width : (h + 1) * width, :].astype(F32) * share[r : r + 1, :]
        mixed[h * width : (h + 1) * width, :] = acc.astype(BF16)
    for z, s in turns:
        copy(z, s).wait()
        (own_ref, other_ref)[s][z] = lax.dot_general(
            mixed[...], held[z, s], (((0,), (0,)), ((), ())), preferred_element_type=F32
        ).astype(BF16)


def project(core, parts, weight, heads, span):
    depth = weight.shape[0]
    zs = weight.shape[1] // span // 2
    rows = parts.shape[2]
    result = pl.BlockSpec((zs, rows, span), lambda i, core: (0, 0, 0))
    return pl.pallas_call(
        functools.partial(project_kernel, heads),
        out_shape=[jax.ShapeDtypeStruct((zs, rows, span), BF16)] * 2,
        grid_spec=pltpu.PrefetchScalarGridSpec(
            num_scalar_prefetch=1,
            grid=(1,),
            in_specs=[
                pl.BlockSpec(parts.shape, lambda i, core: (0, 0, 0)),
                pl.BlockSpec(memory_space=pl.ANY),
            ],
            out_specs=[result, result],
            scratch_shapes=[
                pltpu.VMEM((depth, rows), BF16),
                pltpu.VMEM((zs, 2, depth, span), BF16),
                pltpu.SemaphoreType.DMA((zs, 2)),
            ],
        ),
        compiler_params=pltpu.CompilerParams(vmem_limit_bytes=14 * 1024 * 1024),
        name="project",
    )(core, parts, in_hbm(weight))


def pair_kernel(z, mine, theirs, own, *others):
    zs = mine.shape[0]
    for d, out in zip((0,) + Z_STEPS, (own,) + others):
        at = lax.rem(z[0] + d, jnp.int32(zs))
        out[...] = (mine[at].astype(F32) + theirs[at].astype(F32)).astype(out.dtype)


def pair(z, mine, theirs):
    shape = mine.shape[1:]
    whole = pl.BlockSpec(mine.shape, lambda i, z: (0, 0, 0))
    return pl.pallas_call(
        pair_kernel,
        out_shape=[jax.ShapeDtypeStruct(shape, F32)]
        + [jax.ShapeDtypeStruct(shape, BF16) for _ in Z_STEPS],
        grid_spec=pltpu.PrefetchScalarGridSpec(
            num_scalar_prefetch=1,
            grid=(1,),
            in_specs=[whole, whole],
            out_specs=[pl.BlockSpec(shape, lambda i, z: (0, 0))] * (1 + len(Z_STEPS)),
        ),
        compiler_params=pltpu.CompilerParams(vmem_limit_bytes=8 * 1024 * 1024),
        name="pair",
    )(z, mine, theirs)


def local(queries, key_states, value_states, block_ids, block_counts, out_weight):
    heads = block_ids.shape[0]
    ranges = lax.axis_size("keys")
    groups = lax.axis_size("heads")
    me = lax.axis_index("heads")
    core = jnp.reshape(me % 2, (1,)).astype(jnp.int32)
    z = jnp.reshape(me // 2, (1,)).astype(jnp.int32)
    span = out_weight.shape[1] // groups
    tiles = key_states.shape[0] // BLOCK
    owned = queries.shape[0] // BLOCK
    side = math.isqrt(ranges)

    def exchange(parts):
        return lax.all_to_all(parts, "keys", split_axis=0, concat_axis=0, tiled=True)

    def finish(got):
        mine, theirs = project(core, got, out_weight, heads, span)
        swap = [(g, g ^ 1) for g in range(groups)]
        own, *others = pair(z, mine, lax.ppermute(theirs, "heads", swap))
        total = own
        for d, piece in zip(Z_STEPS, others):
            pairs = [(g, (g + 2 * d) % groups) for g in range(groups)]
            total = total + lax.ppermute(piece, "heads", pairs).astype(F32)
        return total.astype(BF16)

    def along(x, axis):
        def pairs(d):
            there = lambda i, j: ((i + d) % side, j) if axis == 0 else (i, (j + d) % side)
            moved = [there(k // side, k % side) for k in range(ranges)]
            return [(k, i * side + j) for k, (i, j) in enumerate(moved)]

        return {d: lax.ppermute(x, "keys", pairs(d)) for d in Z_STEPS}

    def line(x, got):
        return [x] + [got[d] for d in range(1, side)]

    middle = queries.shape[1] // 2
    left, right = queries[:, :middle], queries[:, middle:]
    left, right = lax.optimization_barrier((left, right))
    halves = line(left, along(left, 0)) + line(right, along(right, 1))
    slot = jnp.reshape(lax.axis_index("keys"), (1,)).astype(jnp.int32)
    entries, starts = plan(slot, block_ids, block_counts, tiles, owned, side)
    *halves, entries, starts = lax.optimization_barrier(halves + [entries, starts])
    far = max(Z_STEPS, key=lambda d: min(d, side - d))
    ready, later = [], []
    for c, (left, right) in enumerate(regroup(halves, side, owned)):
        left, right = lax.optimization_barrier((left, right))
        got = [along(left, 1), along(right, 0)]
        later.append((left, right, got))
        if c == 0:
            ready += [g[d] for g in got for d in Z_STEPS]
        else:
            ready += [g[far] for g in got]
    ready = iter(lax.optimization_barrier(ready))
    for c, (_, _, got) in enumerate(later):
        for g in got:
            g.update({d: next(ready) for d in (Z_STEPS if c == 0 else (far,))})

    def source(c):
        left, right, (up, across) = later[c]
        pieces = line(left, up) + line(right, across)
        pieces = [x.reshape(side, BLOCK, middle) for x in pieces]
        return pieces if c == 0 else [in_hbm(x) for x in pieces]

    lower = [[(i, h) for i in range(side)] for h in range(heads // 2)]
    upper = [[(side + i, h) for i in range(side)] for h in range(heads // 2)]

    outs = []
    for c in range(owned):
        parts = attend(c, entries, starts, source(c), lower + upper, key_states, value_states)
        if c == 0:
            near = [g[d] for _, _, got in later[1:] for g in got for d in Z_STEPS if d != far]
            parts, *near = lax.optimization_barrier([parts] + near)
            near = iter(near)
            for _, _, got in later[1:]:
                for g in got:
                    g.update({d: next(near) for d in Z_STEPS if d != far})
        got = exchange(parts)
        if outs:
            got, outs[-1] = lax.optimization_barrier((got, outs[-1]))
        outs.append(finish(got))
    return jnp.concatenate(outs)


def solution(mesh):
    in_specs = (
        P("keys", "heads"),
        P("keys", "heads"),
        P("keys", "heads"),
        P("heads", "keys"),
        P("heads", "keys"),
        P("heads", None),
    )
    return jax.shard_map(
        local, mesh=mesh, in_specs=in_specs, out_specs=P("keys", "heads"), check_vma=False
    )
```

```python
import functools
import math

import jax
import jax.numpy as jnp
from jax import lax
from jax.experimental import pallas as pl
from jax.experimental.pallas import tpu as pltpu
from jax.sharding import PartitionSpec as P

BLOCK = 128
UNROLL = 16
PLAN_UNROLL = 8
CHUNK_BIT = 28
STAT_ROWS = 16
ABSENT = -3.0e38
Z_STEPS = (1, 3, 2)
F32 = jnp.float32
BF16 = jnp.bfloat16


def split3(x):
    high = x.astype(BF16).astype(F32)
    rest = x - high
    middle = rest.astype(BF16).astype(F32)
    return high, middle, rest - middle


def plan_kernel(owned, codes, counts, entries, starts):
    heads = codes.shape[0]

    def over_head(h, at):
        for c in range(owned):
            starts[c, h] = at[c]
        count = counts[h, 0]

        def some(step, at):
            for u in range(PLAN_UNROLL):
                j = step * PLAN_UNROLL + u
                code = codes[h, j]
                chunk = lax.shift_right_logical(code, CHUNK_BIT)
                place = at[0]
                for c in range(1, owned):
                    place = jnp.where(chunk == c, at[c], place)
                entries[chunk, place] = code
                live = j < count
                at = tuple(
                    a + jnp.where(live & (chunk == c), 1, 0) for c, a in enumerate(at)
                )
            return at

        return lax.fori_loop(0, lax.div(count + PLAN_UNROLL - 1, PLAN_UNROLL), some, at)

    at = lax.fori_loop(0, heads, over_head, (jnp.int32(0),) * owned)
    for c in range(owned):
        starts[c, heads] = at[c]


def plan(me, ids, counts, tiles, owned, side):
    heads, slots = ids.shape
    query, tile = ids // tiles, ids % tiles
    owner, chunk = query // owned, query % owned
    dx = (me // side - owner // side) % side
    dy = (me % side - owner % side) % side
    head = jnp.arange(heads, dtype=jnp.int32)[:, None]
    position = jnp.where(head < heads // 2, dy * side + dx, dx * side + dy)
    codes = (((chunk * 16 + head) * 256 + owner) * 256 + position) * 256 + tile
    smem = pl.BlockSpec(memory_space=pltpu.SMEM)
    return pl.pallas_call(
        functools.partial(plan_kernel, owned),
        out_shape=(
            jax.ShapeDtypeStruct((owned, heads * slots + PLAN_UNROLL), jnp.int32),
            jax.ShapeDtypeStruct((owned, heads + 1), jnp.int32),
        ),
        in_specs=[smem, smem],
        out_specs=(smem, smem),
        compiler_params=pltpu.CompilerParams(vmem_limit_bytes=1024 * 1024),
        name="plan",
    )(codes, counts)


def regroup_kernel(side, *refs):
    pieces, lines = refs[: 2 * side], refs[2 * side :]
    for n, line in enumerate(lines):
        chunk, half = divmod(n, 2)
        for d in range(side):
            piece = pieces[half * side + d]
            line[d * BLOCK : (d + 1) * BLOCK] = piece[chunk * BLOCK : (chunk + 1) * BLOCK]


def regroup(halves, side, owned):
    vmem = pl.BlockSpec(memory_space=pltpu.VMEM)
    line = jax.ShapeDtypeStruct((side * BLOCK, halves[0].shape[1]), BF16)
    lines = pl.pallas_call(
        functools.partial(regroup_kernel, side),
        out_shape=[line] * (2 * owned),
        in_specs=[vmem] * (2 * side),
        out_specs=[vmem] * (2 * owned),
        compiler_params=pltpu.CompilerParams(vmem_limit_bytes=8 * 1024 * 1024),
        name="regroup",
    )(*halves)
    return [(lines[2 * c], lines[2 * c + 1]) for c in range(owned)]


def attend_kernel(chunk, sources, entries, starts, *refs):
    blocks = 1 + max(i for pieces in sources for i, _ in pieces)
    q_hbm = refs[:blocks]
    k_hbm, v_hbm, out_ref, qs, ks, vs, acc, top, den, stats, sems = refs[blocks:]
    heads, owners, _, width = qs.shape
    scale = width**-0.5 * math.log2(math.e)

    def copies(h):
        moves = [(k_hbm.at[:, h * width : (h + 1) * width], ks.at[h])]
        moves.append((v_hbm.at[:, h * width : (h + 1) * width], vs.at[h]))
        for n, (i, lane) in enumerate(sources[h]):
            blocks = q_hbm[i].shape[0]
            src = q_hbm[i].at[:, :, lane * width : (lane + 1) * width]
            moves.append((src, qs.at[h, n * blocks : (n + 1) * blocks]))
        return [
            pltpu.make_async_copy(src, dst, sems.at[h, i]) for i, (src, dst) in enumerate(moves)
        ]

    for h in range(heads):
        for copy in copies(h):
            copy.start()
    acc[...] = jnp.zeros_like(acc)
    den[...] = jnp.zeros_like(den)
    top[...] = jnp.full_like(top, -jnp.inf)
    count = starts[chunk, heads]
    groups = lax.div(count + UNROLL - 1, jnp.int32(UNROLL))
    opens = [lax.div(starts[chunk, h], jnp.int32(UNROLL)) for h in range(heads)]

    def group(step, carry):
        for h in range(heads):

            @pl.when(step == opens[h])
            def _():
                for copy in copies(h):
                    copy.wait()

        slots = []
        for u in range(UNROLL):
            j = step * UNROLL + u
            live = j < count
            entry = jnp.where(live, entries[chunk, j], 0)
            head = lax.bitwise_and(lax.shift_right_logical(entry, 24), 15)
            owner = lax.bitwise_and(lax.shift_right_logical(entry, 16), 255)
            position = lax.bitwise_and(lax.shift_right_logical(entry, 8), 255)
            tile = lax.bitwise_and(entry, 255)
            slot = jnp.where(live, head * owners + owner, heads * owners)
            slots.append((slot, head, position, tile))

        def rows(i):
            return pl.ds(pl.multiple_of(i * BLOCK, BLOCK), BLOCK)

        scores = [
            lax.dot_general(
                ks[head, rows(tile), :],
                qs[head, position],
                (((1,), (1,)), ((), ())),
                preferred_element_type=F32,
            )
            for _, head, position, tile in slots
        ]
        scores = [s * scale for s in scores]
        tops = [jnp.max(s, axis=0, keepdims=True) for s in scores]
        steps = []
        for (slot, _, _, _), m in zip(slots, tops):
            row = pl.ds(slot, 1)
            old = top[row, :]
            new = jnp.maximum(old, m)
            top[row, :] = new
            steps.append((new, jnp.exp2(old - new)))
        parts = []
        for (slot, head, _, tile), s, (new, _) in zip(slots, scores, steps):
            p = jnp.exp2(s - new)
            d = jnp.sum(p, axis=0, keepdims=True)
            o = lax.dot_general(
                vs[head, rows(tile), :],
                p.astype(BF16),
                (((0,), (0,)), ((), ())),
                preferred_element_type=F32,
            )
            parts.append((d, o))
        for (slot, _, _, _), (_, keep), (d, o) in zip(slots, steps, parts):
            row = pl.ds(slot, 1)
            den[row, :] = den[row, :] * keep + d
            acc[slot] = acc[slot] * keep + o
        return carry

    lax.fori_loop(0, groups, group, 0)
    for h in range(heads):

        @pl.when(opens[h] >= groups)
        def _():
            for copy in copies(h):
                copy.wait()

    used = heads * owners
    total = den[0:used, :]
    listed = total > 0
    safe = jnp.where(listed, total, 1.0)
    level = jnp.where(listed, top[0:used, :] + jnp.log2(safe), ABSENT)
    den[0:used, :] = jnp.where(listed, 1.0 / safe, 0.0)
    for h in range(heads):
        for q in range(owners):
            at = h * owners + q
            out_ref[q, h * width : (h + 1) * width, :] = (acc[at] * den[at : at + 1, :]).astype(BF16)
        for i, piece in enumerate(split3(level[h * owners : (h + 1) * owners])):
            stats[3 * h + i] = piece
    first = out_ref.shape[1] - STAT_ROWS
    for q in range(owners):
        rows = [stats[i, q : q + 1, :] for i in range(3 * heads)]
        rows.append(jnp.zeros((STAT_ROWS - 3 * heads, BLOCK), F32))
        out_ref[q, first:, :] = jnp.concatenate(rows, axis=0).astype(BF16)


def in_hbm(x):
    return pltpu.with_memory_space_constraint(x, pltpu.HBM)


def attend(chunk, entries, starts, queries, sources, keys, values):
    heads = len(sources)
    width = keys.shape[1] // heads
    owners = sum(queries[i].shape[0] for i, _ in sources[0])
    smem = pl.BlockSpec(memory_space=pltpu.SMEM)
    hbm = pl.BlockSpec(memory_space=pl.ANY)
    lines = -(-(heads * owners + 1) // 8) * 8
    return pl.pallas_call(
        functools.partial(attend_kernel, chunk, sources),
        out_shape=jax.ShapeDtypeStruct((owners, heads * width + STAT_ROWS, BLOCK), BF16),
        in_specs=[smem, smem] + [hbm] * (len(queries) + 2),
        scratch_shapes=[
            pltpu.VMEM((heads, owners, BLOCK, width), BF16),
            pltpu.VMEM((heads, keys.shape[0], width), BF16),
            pltpu.VMEM((heads, values.shape[0], width), BF16),
            pltpu.VMEM((heads * owners + 1, width, BLOCK), F32),
            pltpu.VMEM((lines, BLOCK), F32),
            pltpu.VMEM((lines, BLOCK), F32),
            pltpu.VMEM((3 * heads, owners, BLOCK), F32),
            pltpu.SemaphoreType.DMA((heads, 2 + max(len(p) for p in sources))),
        ],
        compiler_params=pltpu.CompilerParams(vmem_limit_bytes=40 * 1024 * 1024),
        name="attend",
    )(entries, starts, *queries, in_hbm(keys), in_hbm(values))


def project_kernel(heads, core, in_ref, weight, own_ref, other_ref, mixed, held, sems):
    ranges, total, rows = in_ref.shape
    width = (total - STAT_ROWS) // heads
    first = total - STAT_ROWS
    zs, _, span = own_ref.shape

    def copy(z, s):
        column = pl.multiple_of((2 * z + jnp.bitwise_xor(core[0], s)) * span, span)
        return pltpu.make_async_copy(
            weight.at[:, pl.ds(column, span)], held.at[z, s], sems.at[z, s]
        )

    turns = [(z, s) for z in range(zs) for s in range(2)]
    for z, s in turns:
        copy(z, s).start()
    stats = in_ref[:, first:, :].astype(F32)
    for h in range(heads):
        level = stats[:, 3 * h, :] + stats[:, 3 * h + 1, :] + stats[:, 3 * h + 2, :]
        share = jnp.exp2(level - jnp.max(level, axis=0, keepdims=True))
        share = share / jnp.sum(share, axis=0, keepdims=True)
        acc = jnp.zeros((width, rows), F32)
        for r in range(ranges):
            acc += in_ref[r, h * width : (h + 1) * width, :].astype(F32) * share[r : r + 1, :]
        mixed[h * width : (h + 1) * width, :] = acc.astype(BF16)
    for z, s in turns:
        copy(z, s).wait()
        (own_ref, other_ref)[s][z] = lax.dot_general(
            mixed[...], held[z, s], (((0,), (0,)), ((), ())), preferred_element_type=F32
        ).astype(BF16)


def project(core, parts, weight, heads, span):
    depth = weight.shape[0]
    zs = weight.shape[1] // span // 2
    rows = parts.shape[2]
    result = pl.BlockSpec((zs, rows, span), lambda i, core: (0, 0, 0))
    return pl.pallas_call(
        functools.partial(project_kernel, heads),
        out_shape=[jax.ShapeDtypeStruct((zs, rows, span), BF16)] * 2,
        grid_spec=pltpu.PrefetchScalarGridSpec(
            num_scalar_prefetch=1,
            grid=(1,),
            in_specs=[
                pl.BlockSpec(parts.shape, lambda i, core: (0, 0, 0)),
                pl.BlockSpec(memory_space=pl.ANY),
            ],
            out_specs=[result, result],
            scratch_shapes=[
                pltpu.VMEM((depth, rows), BF16),
                pltpu.VMEM((zs, 2, depth, span), BF16),
                pltpu.SemaphoreType.DMA((zs, 2)),
            ],
        ),
        compiler_params=pltpu.CompilerParams(vmem_limit_bytes=14 * 1024 * 1024),
        name="project",
    )(core, parts, in_hbm(weight))


def pair_kernel(z, mine, theirs, own, *others):
    zs = mine.shape[0]
    for d, out in zip((0,) + Z_STEPS, (own,) + others):
        at = lax.rem(z[0] + d, jnp.int32(zs))
        out[...] = (mine[at].astype(F32) + theirs[at].astype(F32)).astype(out.dtype)


def pair(z, mine, theirs):
    shape = mine.shape[1:]
    whole = pl.BlockSpec(mine.shape, lambda i, z: (0, 0, 0))
    return pl.pallas_call(
        pair_kernel,
        out_shape=[jax.ShapeDtypeStruct(shape, F32)]
        + [jax.ShapeDtypeStruct(shape, BF16) for _ in Z_STEPS],
        grid_spec=pltpu.PrefetchScalarGridSpec(
            num_scalar_prefetch=1,
            grid=(1,),
            in_specs=[whole, whole],
            out_specs=[pl.BlockSpec(shape, lambda i, z: (0, 0))] * (1 + len(Z_STEPS)),
        ),
        compiler_params=pltpu.CompilerParams(vmem_limit_bytes=8 * 1024 * 1024),
        name="pair",
    )(z, mine, theirs)


def local(queries, key_states, value_states, block_ids, block_counts, out_weight):
    heads = block_ids.shape[0]
    ranges = lax.axis_size("keys")
    groups = lax.axis_size("heads")
    me = lax.axis_index("heads")
    core = jnp.reshape(me % 2, (1,)).astype(jnp.int32)
    z = jnp.reshape(me // 2, (1,)).astype(jnp.int32)
    span = out_weight.shape[1] // groups
    tiles = key_states.shape[0] // BLOCK
    owned = queries.shape[0] // BLOCK
    side = math.isqrt(ranges)

    def exchange(parts):
        return lax.all_to_all(parts, "keys", split_axis=0, concat_axis=0, tiled=True)

    def finish(got):
        mine, theirs = project(core, got, out_weight, heads, span)
        swap = [(g, g ^ 1) for g in range(groups)]
        own, *others = pair(z, mine, lax.ppermute(theirs, "heads", swap))
        total = own
        for d, piece in zip(Z_STEPS, others):
            pairs = [(g, (g + 2 * d) % groups) for g in range(groups)]
            total = total + lax.ppermute(piece, "heads", pairs).astype(F32)
        return total.astype(BF16)

    def along(x, axis):
        def pairs(d):
            there = lambda i, j: ((i + d) % side, j) if axis == 0 else (i, (j + d) % side)
            moved = [there(k // side, k % side) for k in range(ranges)]
            return [(k, i * side + j) for k, (i, j) in enumerate(moved)]

        return {d: lax.ppermute(x, "keys", pairs(d)) for d in Z_STEPS}

    def line(x, got):
        return [x] + [got[d] for d in range(1, side)]

    middle = queries.shape[1] // 2
    left, right = queries[:, :middle], queries[:, middle:]
    left, right = lax.optimization_barrier((left, right))
    halves = line(left, along(left, 0)) + line(right, along(right, 1))
    slot = jnp.reshape(lax.axis_index("keys"), (1,)).astype(jnp.int32)
    entries, starts = plan(slot, block_ids, block_counts, tiles, owned, side)
    *halves, entries, starts = lax.optimization_barrier(halves + [entries, starts])
    far = max(Z_STEPS, key=lambda d: min(d, side - d))
    ready, later = [], []
    for c, (left, right) in enumerate(regroup(halves, side, owned)):
        left, right = lax.optimization_barrier((left, right))
        got = [along(left, 1), along(right, 0)]
        later.append((left, right, got))
        if c == 0:
            ready += [g[d] for g in got for d in Z_STEPS]
        else:
            ready += [g[far] for g in got]
    ready = iter(lax.optimization_barrier(ready))
    for c, (_, _, got) in enumerate(later):
        for g in got:
            g.update({d: next(ready) for d in (Z_STEPS if c == 0 else (far,))})

    def source(c):
        left, right, (up, across) = later[c]
        pieces = line(left, up) + line(right, across)
        pieces = [x.reshape(side, BLOCK, middle) for x in pieces]
        return pieces if c == 0 else [in_hbm(x) for x in pieces]

    lower = [[(i, h) for i in range(side)] for h in range(heads // 2)]
    upper = [[(side + i, h) for i in range(side)] for h in range(heads // 2)]

    outs = []
    for c in range(owned):
        parts = attend(c, entries, starts, source(c), lower + upper, key_states, value_states)
        if c == 0:
            near = [g[d] for _, _, got in later[1:] for g in got for d in Z_STEPS if d != far]
            parts, *near = lax.optimization_barrier([parts] + near)
            near = iter(near)
            for _, _, got in later[1:]:
                for g in got:
                    g.update({d: next(near) for d in Z_STEPS if d != far})
        got = exchange(parts)
        if c < owned - 1:
            got = in_hbm(got)
        if outs:
            got, outs[-1] = lax.optimization_barrier((got, outs[-1]))
        outs.append(finish(got))
    return jnp.concatenate(outs)


def solution(mesh):
    in_specs = (
        P("keys", "heads"),
        P("keys", "heads"),
        P("keys", "heads"),
        P("heads", "keys"),
        P("heads", "keys"),
        P("heads", None),
    )
    return jax.shard_map(
        local, mesh=mesh, in_specs=in_specs, out_specs=P("keys", "heads"), check_vma=False
    )
```

```python
import functools
import math

import jax
import jax.numpy as jnp
from jax import lax
from jax.experimental import pallas as pl
from jax.experimental.pallas import tpu as pltpu
from jax.sharding import PartitionSpec as P

BLOCK = 128
UNROLL = 24
PLAN_UNROLL = 8
CHUNK_BIT = 28
STAT_ROWS = 16
ABSENT = -3.0e38
Z_STEPS = (1, 3, 2)
F32 = jnp.float32
BF16 = jnp.bfloat16


def split3(x):
    high = x.astype(BF16).astype(F32)
    rest = x - high
    middle = rest.astype(BF16).astype(F32)
    return high, middle, rest - middle


def plan_kernel(owned, codes, counts, entries, starts):
    heads = codes.shape[0]

    def over_head(h, at):
        for c in range(owned):
            starts[c, h] = at[c]
        count = counts[h, 0]

        def some(step, at):
            for u in range(PLAN_UNROLL):
                j = step * PLAN_UNROLL + u
                code = codes[h, j]
                chunk = lax.shift_right_logical(code, CHUNK_BIT)
                place = at[0]
                for c in range(1, owned):
                    place = jnp.where(chunk == c, at[c], place)
                entries[chunk, place] = code
                live = j < count
                at = tuple(
                    a + jnp.where(live & (chunk == c), 1, 0) for c, a in enumerate(at)
                )
            return at

        return lax.fori_loop(0, lax.div(count + PLAN_UNROLL - 1, PLAN_UNROLL), some, at)

    at = lax.fori_loop(0, heads, over_head, (jnp.int32(0),) * owned)
    for c in range(owned):
        starts[c, heads] = at[c]


def plan(me, ids, counts, tiles, owned, side):
    heads, slots = ids.shape
    query, tile = ids // tiles, ids % tiles
    owner, chunk = query // owned, query % owned
    dx = (me // side - owner // side) % side
    dy = (me % side - owner % side) % side
    head = jnp.arange(heads, dtype=jnp.int32)[:, None]
    position = jnp.where(head < heads // 2, dy * side + dx, dx * side + dy)
    codes = (((chunk * 16 + head) * 256 + owner) * 256 + position) * 256 + tile
    smem = pl.BlockSpec(memory_space=pltpu.SMEM)
    return pl.pallas_call(
        functools.partial(plan_kernel, owned),
        out_shape=(
            jax.ShapeDtypeStruct((owned, heads * slots + PLAN_UNROLL), jnp.int32),
            jax.ShapeDtypeStruct((owned, heads + 1), jnp.int32),
        ),
        in_specs=[smem, smem],
        out_specs=(smem, smem),
        compiler_params=pltpu.CompilerParams(vmem_limit_bytes=1024 * 1024),
        name="plan",
    )(codes, counts)


def regroup_kernel(side, *refs):
    pieces, lines = refs[: 2 * side], refs[2 * side :]
    for n, line in enumerate(lines):
        chunk, half = divmod(n, 2)
        for d in range(side):
            piece = pieces[half * side + d]
            line[d * BLOCK : (d + 1) * BLOCK] = piece[chunk * BLOCK : (chunk + 1) * BLOCK]


def regroup(halves, side, owned):
    vmem = pl.BlockSpec(memory_space=pltpu.VMEM)
    line = jax.ShapeDtypeStruct((side * BLOCK, halves[0].shape[1]), BF16)
    lines = pl.pallas_call(
        functools.partial(regroup_kernel, side),
        out_shape=[line] * (2 * owned),
        in_specs=[vmem] * (2 * side),
        out_specs=[vmem] * (2 * owned),
        compiler_params=pltpu.CompilerParams(vmem_limit_bytes=8 * 1024 * 1024),
        name="regroup",
    )(*halves)
    return [(lines[2 * c], lines[2 * c + 1]) for c in range(owned)]


def attend_kernel(chunk, sources, entries, starts, *refs):
    blocks = 1 + max(i for pieces in sources for i, _ in pieces)
    q_hbm = refs[:blocks]
    k_hbm, v_hbm, out_ref, qs, ks, vs, acc, top, den, stats, sems = refs[blocks:]
    heads, owners, _, width = qs.shape
    scale = width**-0.5 * math.log2(math.e)

    def copies(h):
        moves = [(k_hbm.at[:, h * width : (h + 1) * width], ks.at[h])]
        moves.append((v_hbm.at[:, h * width : (h + 1) * width], vs.at[h]))
        for n, (i, lane) in enumerate(sources[h]):
            blocks = q_hbm[i].shape[0]
            src = q_hbm[i].at[:, :, lane * width : (lane + 1) * width]
            moves.append((src, qs.at[h, n * blocks : (n + 1) * blocks]))
        return [
            pltpu.make_async_copy(src, dst, sems.at[h, i]) for i, (src, dst) in enumerate(moves)
        ]

    for h in range(heads):
        for copy in copies(h):
            copy.start()
    acc[...] = jnp.zeros_like(acc)
    den[...] = jnp.zeros_like(den)
    top[...] = jnp.full_like(top, -jnp.inf)
    count = starts[chunk, heads]
    groups = lax.div(count + UNROLL - 1, jnp.int32(UNROLL))
    opens = [lax.div(starts[chunk, h], jnp.int32(UNROLL)) for h in range(heads)]

    def group(step, carry):
        for h in range(heads):

            @pl.when(step == opens[h])
            def _():
                for copy in copies(h):
                    copy.wait()

        slots = []
        for u in range(UNROLL):
            j = step * UNROLL + u
            live = j < count
            entry = jnp.where(live, entries[chunk, j], 0)
            head = lax.bitwise_and(lax.shift_right_logical(entry, 24), 15)
            owner = lax.bitwise_and(lax.shift_right_logical(entry, 16), 255)
            position = lax.bitwise_and(lax.shift_right_logical(entry, 8), 255)
            tile = lax.bitwise_and(entry, 255)
            slot = jnp.where(live, head * owners + owner, heads * owners)
            slots.append((slot, head, position, tile))

        def rows(i):
            return pl.ds(pl.multiple_of(i * BLOCK, BLOCK), BLOCK)

        scores = [
            lax.dot_general(
                ks[head, rows(tile), :],
                qs[head, position],
                (((1,), (1,)), ((), ())),
                preferred_element_type=F32,
            )
            for _, head, position, tile in slots
        ]
        scores = [s * scale for s in scores]
        tops = [jnp.max(s, axis=0, keepdims=True) for s in scores]
        steps = []
        for (slot, _, _, _), m in zip(slots, tops):
            row = pl.ds(slot, 1)
            old = top[row, :]
            new = jnp.maximum(old, m)
            top[row, :] = new
            steps.append((new, jnp.exp2(old - new)))
        parts = []
        for (slot, head, _, tile), s, (new, _) in zip(slots, scores, steps):
            p = jnp.exp2(s - new)
            d = jnp.sum(p, axis=0, keepdims=True)
            o = lax.dot_general(
                vs[head, rows(tile), :],
                p.astype(BF16),
                (((0,), (0,)), ((), ())),
                preferred_element_type=F32,
            )
            parts.append((d, o))
        for (slot, _, _, _), (_, keep), (d, o) in zip(slots, steps, parts):
            row = pl.ds(slot, 1)
            den[row, :] = den[row, :] * keep + d
            acc[slot] = acc[slot] * keep + o
        return carry

    lax.fori_loop(0, groups, group, 0)
    for h in range(heads):

        @pl.when(opens[h] >= groups)
        def _():
            for copy in copies(h):
                copy.wait()

    used = heads * owners
    total = den[0:used, :]
    listed = total > 0
    safe = jnp.where(listed, total, 1.0)
    level = jnp.where(listed, top[0:used, :] + jnp.log2(safe), ABSENT)
    den[0:used, :] = jnp.where(listed, 1.0 / safe, 0.0)
    for h in range(heads):
        for q in range(owners):
            at = h * owners + q
            out_ref[q, h * width : (h + 1) * width, :] = (acc[at] * den[at : at + 1, :]).astype(BF16)
        for i, piece in enumerate(split3(level[h * owners : (h + 1) * owners])):
            stats[3 * h + i] = piece
    first = out_ref.shape[1] - STAT_ROWS
    for q in range(owners):
        rows = [stats[i, q : q + 1, :] for i in range(3 * heads)]
        rows.append(jnp.zeros((STAT_ROWS - 3 * heads, BLOCK), F32))
        out_ref[q, first:, :] = jnp.concatenate(rows, axis=0).astype(BF16)


def in_hbm(x):
    return pltpu.with_memory_space_constraint(x, pltpu.HBM)


def attend(chunk, entries, starts, queries, sources, keys, values):
    heads = len(sources)
    width = keys.shape[1] // heads
    owners = sum(queries[i].shape[0] for i, _ in sources[0])
    smem = pl.BlockSpec(memory_space=pltpu.SMEM)
    hbm = pl.BlockSpec(memory_space=pl.ANY)
    lines = -(-(heads * owners + 1) // 8) * 8
    return pl.pallas_call(
        functools.partial(attend_kernel, chunk, sources),
        out_shape=jax.ShapeDtypeStruct((owners, heads * width + STAT_ROWS, BLOCK), BF16),
        in_specs=[smem, smem] + [hbm] * (len(queries) + 2),
        scratch_shapes=[
            pltpu.VMEM((heads, owners, BLOCK, width), BF16),
            pltpu.VMEM((heads, keys.shape[0], width), BF16),
            pltpu.VMEM((heads, values.shape[0], width), BF16),
            pltpu.VMEM((heads * owners + 1, width, BLOCK), F32),
            pltpu.VMEM((lines, BLOCK), F32),
            pltpu.VMEM((lines, BLOCK), F32),
            pltpu.VMEM((3 * heads, owners, BLOCK), F32),
            pltpu.SemaphoreType.DMA((heads, 2 + max(len(p) for p in sources))),
        ],
        compiler_params=pltpu.CompilerParams(vmem_limit_bytes=40 * 1024 * 1024),
        name="attend",
    )(entries, starts, *queries, in_hbm(keys), in_hbm(values))


def project_kernel(heads, core, in_ref, weight, own_ref, other_ref, mixed, held, sems):
    ranges, total, rows = in_ref.shape
    width = (total - STAT_ROWS) // heads
    first = total - STAT_ROWS
    zs, _, span = own_ref.shape

    def copy(z, s):
        column = pl.multiple_of((2 * z + jnp.bitwise_xor(core[0], s)) * span, span)
        return pltpu.make_async_copy(
            weight.at[:, pl.ds(column, span)], held.at[z, s], sems.at[z, s]
        )

    turns = [(z, s) for z in range(zs) for s in range(2)]
    for z, s in turns:
        copy(z, s).start()
    stats = in_ref[:, first:, :].astype(F32)
    for h in range(heads):
        level = stats[:, 3 * h, :] + stats[:, 3 * h + 1, :] + stats[:, 3 * h + 2, :]
        share = jnp.exp2(level - jnp.max(level, axis=0, keepdims=True))
        share = share / jnp.sum(share, axis=0, keepdims=True)
        acc = jnp.zeros((width, rows), F32)
        for r in range(ranges):
            acc += in_ref[r, h * width : (h + 1) * width, :].astype(F32) * share[r : r + 1, :]
        mixed[h * width : (h + 1) * width, :] = acc.astype(BF16)
    for z, s in turns:
        copy(z, s).wait()
        (own_ref, other_ref)[s][z] = lax.dot_general(
            mixed[...], held[z, s], (((0,), (0,)), ((), ())), preferred_element_type=F32
        ).astype(BF16)


def project(core, parts, weight, heads, span):
    depth = weight.shape[0]
    zs = weight.shape[1] // span // 2
    rows = parts.shape[2]
    result = pl.BlockSpec((zs, rows, span), lambda i, core: (0, 0, 0))
    return pl.pallas_call(
        functools.partial(project_kernel, heads),
        out_shape=[jax.ShapeDtypeStruct((zs, rows, span), BF16)] * 2,
        grid_spec=pltpu.PrefetchScalarGridSpec(
            num_scalar_prefetch=1,
            grid=(1,),
            in_specs=[
                pl.BlockSpec(parts.shape, lambda i, core: (0, 0, 0)),
                pl.BlockSpec(memory_space=pl.ANY),
            ],
            out_specs=[result, result],
            scratch_shapes=[
                pltpu.VMEM((depth, rows), BF16),
                pltpu.VMEM((zs, 2, depth, span), BF16),
                pltpu.SemaphoreType.DMA((zs, 2)),
            ],
        ),
        compiler_params=pltpu.CompilerParams(vmem_limit_bytes=14 * 1024 * 1024),
        name="project",
    )(core, parts, in_hbm(weight))


def pair_kernel(z, mine, theirs, own, *others):
    zs = mine.shape[0]
    for d, out in zip((0,) + Z_STEPS, (own,) + others):
        at = lax.rem(z[0] + d, jnp.int32(zs))
        out[...] = (mine[at].astype(F32) + theirs[at].astype(F32)).astype(out.dtype)


def pair(z, mine, theirs):
    shape = mine.shape[1:]
    whole = pl.BlockSpec(mine.shape, lambda i, z: (0, 0, 0))
    return pl.pallas_call(
        pair_kernel,
        out_shape=[jax.ShapeDtypeStruct(shape, F32)]
        + [jax.ShapeDtypeStruct(shape, BF16) for _ in Z_STEPS],
        grid_spec=pltpu.PrefetchScalarGridSpec(
            num_scalar_prefetch=1,
            grid=(1,),
            in_specs=[whole, whole],
            out_specs=[pl.BlockSpec(shape, lambda i, z: (0, 0))] * (1 + len(Z_STEPS)),
        ),
        compiler_params=pltpu.CompilerParams(vmem_limit_bytes=8 * 1024 * 1024),
        name="pair",
    )(z, mine, theirs)


def local(queries, key_states, value_states, block_ids, block_counts, out_weight):
    heads = block_ids.shape[0]
    ranges = lax.axis_size("keys")
    groups = lax.axis_size("heads")
    me = lax.axis_index("heads")
    core = jnp.reshape(me % 2, (1,)).astype(jnp.int32)
    z = jnp.reshape(me // 2, (1,)).astype(jnp.int32)
    span = out_weight.shape[1] // groups
    tiles = key_states.shape[0] // BLOCK
    owned = queries.shape[0] // BLOCK
    side = math.isqrt(ranges)

    def exchange(parts):
        return lax.all_to_all(parts, "keys", split_axis=0, concat_axis=0, tiled=True)

    def finish(got):
        mine, theirs = project(core, got, out_weight, heads, span)
        swap = [(g, g ^ 1) for g in range(groups)]
        own, *others = pair(z, mine, lax.ppermute(theirs, "heads", swap))
        total = own
        for d, piece in zip(Z_STEPS, others):
            pairs = [(g, (g + 2 * d) % groups) for g in range(groups)]
            total = total + lax.ppermute(piece, "heads", pairs).astype(F32)
        return total.astype(BF16)

    def along(x, axis):
        def pairs(d):
            there = lambda i, j: ((i + d) % side, j) if axis == 0 else (i, (j + d) % side)
            moved = [there(k // side, k % side) for k in range(ranges)]
            return [(k, i * side + j) for k, (i, j) in enumerate(moved)]

        return {d: lax.ppermute(x, "keys", pairs(d)) for d in Z_STEPS}

    def line(x, got):
        return [x] + [got[d] for d in range(1, side)]

    middle = queries.shape[1] // 2
    left, right = queries[:, :middle], queries[:, middle:]
    left, right = lax.optimization_barrier((left, right))
    halves = line(left, along(left, 0)) + line(right, along(right, 1))
    slot = jnp.reshape(lax.axis_index("keys"), (1,)).astype(jnp.int32)
    entries, starts = plan(slot, block_ids, block_counts, tiles, owned, side)
    *halves, entries, starts = lax.optimization_barrier(halves + [entries, starts])
    far = max(Z_STEPS, key=lambda d: min(d, side - d))
    ready, later = [], []
    for c, (left, right) in enumerate(regroup(halves, side, owned)):
        left, right = lax.optimization_barrier((left, right))
        got = [along(left, 1), along(right, 0)]
        later.append((left, right, got))
        if c == 0:
            ready += [g[d] for g in got for d in Z_STEPS]
        else:
            ready += [g[far] for g in got]
    ready = iter(lax.optimization_barrier(ready))
    for c, (_, _, got) in enumerate(later):
        for g in got:
            g.update({d: next(ready) for d in (Z_STEPS if c == 0 else (far,))})

    def source(c):
        left, right, (up, across) = later[c]
        pieces = line(left, up) + line(right, across)
        pieces = [x.reshape(side, BLOCK, middle) for x in pieces]
        return pieces if c == 0 else [in_hbm(x) for x in pieces]

    lower = [[(i, h) for i in range(side)] for h in range(heads // 2)]
    upper = [[(side + i, h) for i in range(side)] for h in range(heads // 2)]

    outs = []
    for c in range(owned):
        parts = attend(c, entries, starts, source(c), lower + upper, key_states, value_states)
        if c == 0:
            near = [g[d] for _, _, got in later[1:] for g in got for d in Z_STEPS if d != far]
            parts, *near = lax.optimization_barrier([parts] + near)
            near = iter(near)
            for _, _, got in later[1:]:
                for g in got:
                    g.update({d: next(near) for d in Z_STEPS if d != far})
        got = exchange(parts)
        if outs:
            got, outs[-1] = lax.optimization_barrier((got, outs[-1]))
        outs.append(finish(got))
    return jnp.concatenate(outs)


def solution(mesh):
    in_specs = (
        P("keys", "heads"),
        P("keys", "heads"),
        P("keys", "heads"),
        P("heads", "keys"),
        P("heads", "keys"),
        P("heads", None),
    )
    return jax.shard_map(
        local, mesh=mesh, in_specs=in_specs, out_specs=P("keys", "heads"), check_vma=False
    )
```
